256 devices in a mesh: cell: 8 (over z_hi, x), seq: 32 (over z_lo, y, core).
Axes of the slice: x: 4, y: 4, z: 8 (z_hi: 2, z_lo: 4; z = z_hi * 4 + z_lo), core: 2. Of those that a mesh axis runs over, the one named last changes fastest.
Arguments:
- features: bfloat16 [8192, 1536], P('seq', 'cell'), may hold values from -6 to 6
- w_qkv: bfloat16 [1536, 768], replicated, may hold values from -0.15625 to 0.15625
- buckets: int32 [8, 64, 16], P('cell', 'seq'), may hold values from 0 to 31
- cell_ids: int32 [8], P('cell'), may hold values from 0 to 31
- bias_table: float32 [32, 32, 2], replicated, may hold values from -8 to 330
- d_attended: bfloat16 [8, 8192, 256], P('cell', 'seq'), may hold values from -6 to 6
Outputs:
- attended: bfloat16 [8, 8192, 256], P('cell', 'seq')
- grad_qkv: float32 [1536, 768], P('cell')
- grad_table: float32 [32, 32, 2], replicated
The draws below stay inside these ranges and needn't reach their ends.
All inputs are finite; a program needn't handle non-finite values.
Results may differ from the reference program's by a relative error of at most 0.02.
Values may be sent and summed in bfloat16 or wider, within the bound.
A program may use at most 64 MiB of HBM per device.

```python
import math
import jax
import jax.numpy as jnp
from jax import lax

D = 1536
HEADS = 2
HD = 128
TILE = 128
BT = 16
NB = 32
TYPES = 32
CELLS = 8
TOKENS = 8192
NTILES = 64


def draw_bias_table(key, part):
    first_key = jax.random.fold_in(jax.random.fold_in(key, 17), 0)
    return jnp.clip(jax.random.normal(first_key, (TYPES, NB, HEADS), jnp.float32), -6.0, 6.0)


def plant(values, own_key, low, largest):
    index_at = [jax.random.randint(jax.random.fold_in(own_key, axis), (), 0, length) for axis, length in enumerate(values.shape)]
    main_axis = values.shape.index(max(values.shape))
    neighbour = index_at[:main_axis] + [(index_at[main_axis] + 1) % values.shape[main_axis]] + index_at[main_axis + 1:]
    return values.at[tuple(index_at)].set(low).at[tuple(neighbour)].set(largest)


def steps_of(stream_key, extent, cuts, low, high):
    level = 1.0
    for axis_at, blocks in cuts:
        draws = jax.random.uniform(jax.random.fold_in(jax.random.fold_in(stream_key, 6), axis_at), (blocks,), jnp.float32, low / len(cuts), high / len(cuts))
        level = level * jnp.repeat(jnp.exp(draws), extent[axis_at] // blocks).reshape((-1,) + (1,) * (len(extent) - 1 - axis_at))
    return level


def gaussian(rng, dims, width, limit, shards=(), kind=jnp.bfloat16):
    loudness = steps_of(rng, dims, shards, -0.22, 0.18) if shards else 1.0
    result = jax.random.normal(rng, dims, jnp.float32) * width * loudness
    return jnp.minimum(jnp.maximum(result, -limit), limit).astype(kind)


def setup_inputs(seed: int = 0) -> dict:
    key_of = jax.random.split(jax.random.key(seed), 7)
    features = gaussian(key_of[0], (TOKENS, D), 1.0, 6.0, ((0, 32), (1, 8)))
    w_qkv = gaussian(key_of[1], (D, 3 * HEADS * HD), D ** -0.5, 0.15625)
    buckets = plant(jax.random.randint(key_of[2], (CELLS, NTILES, BT), 0, NB), jax.random.fold_in(key_of[2], 1), 0, NB - 1).astype(jnp.int32)
    cell_ids = plant(jax.random.randint(key_of[3], (CELLS,), 0, TYPES), jax.random.fold_in(key_of[3], 1), 0, TYPES - 1).astype(jnp.int32)
    bias_table = draw_bias_table(jax.random.fold_in(key_of[6], 71), 0)
    d_attended = gaussian(key_of[5], (CELLS, TOKENS, HEADS * HD), 1.0, 6.0, ((0, 8), (1, 32)))
    return {"features": features, "w_qkv": w_qkv, "buckets": buckets, "cell_ids": cell_ids, "bias_table": bias_table, "d_attended": d_attended}


def tile_bias(bucket_rows, table_row, query_tiles, key_first, key_count, tile_total):
    band_width = bucket_rows.shape[1]
    middle = band_width // 2
    key_tiles = (key_first + jnp.arange(key_count, dtype=jnp.int32)) // TILE
    offsets = key_tiles[None, :] - query_tiles[:, None] + middle
    key_valid = (key_tiles >= 0) & (key_tiles < tile_total)
    query_valid = (query_tiles >= 0) & (query_tiles < tile_total)
    inside = (offsets >= 0) & (offsets < band_width) & key_valid[None, :] & query_valid[:, None]
    matches = offsets[:, :, None] == jnp.arange(band_width, dtype=jnp.int32)[None, None, :]
    bucket_ids = lax.optimization_barrier(jnp.sum(jnp.where(matches, bucket_rows[:, None, :], 0), axis=2))
    levels = table_row.shape[0]
    onehot = (bucket_ids[:, :, None] == jnp.arange(levels, dtype=jnp.int32)[None, None, :]).astype(jnp.float32)
    bias_terms = jnp.einsum('qkb,bh->qhk', onehot, table_row, precision=lax.Precision.HIGHEST)
    return (bias_terms, inside, onehot)

def band_scores(query_rows, key_rows, bias_terms, inside, factor):
    raw_scores = jnp.einsum('qhd,khd->qhk', query_rows.astype(jnp.float32), key_rows.astype(jnp.float32))
    tile_count = bias_terms.shape[0]
    shaped = raw_scores.reshape(tile_count, TILE, raw_scores.shape[1], raw_scores.shape[2]) * factor
    shaped = shaped + bias_terms[:, None]
    keep_mask = jnp.broadcast_to(inside[:, None, None, :], shaped.shape)
    shaped = jnp.where(keep_mask, shaped, -1e+30)
    return (shaped.reshape(raw_scores.shape), keep_mask.reshape(raw_scores.shape))

def reference(features, w_qkv, buckets, cell_ids, bias_table, d_attended):
    total_rows = features.shape[0]
    tile_total = total_rows // TILE
    inner_width = HEADS * HD
    factor = 1.0 / math.sqrt(HD)
    half_band = BT * TILE // 2
    projected = jnp.dot(features, w_qkv, preferred_element_type=jnp.float32).astype(jnp.bfloat16)
    queries = projected[:, :inner_width].reshape(total_rows, HEADS, HD)
    all_keys = projected[:, inner_width:2 * inner_width].reshape(total_rows, HEADS, HD)
    all_values = projected[:, 2 * inner_width:].reshape(total_rows, HEADS, HD)
    padded_keys = jnp.pad(all_keys, ((half_band, half_band), (0, 0), (0, 0)))
    padded_values = jnp.pad(all_values, ((half_band, half_band), (0, 0), (0, 0)))
    padded_total = total_rows + 2 * half_band
    block_rows = math.gcd(total_rows, 512)
    block_count = total_rows // block_rows
    tiles_block = block_rows // TILE
    span_rows = block_rows + 2 * half_band
    query_grad = jnp.zeros((total_rows, HEADS, HD), jnp.float32)
    key_grad = jnp.zeros((total_rows, HEADS, HD), jnp.float32)
    value_grad = jnp.zeros((total_rows, HEADS, HD), jnp.float32)
    grad_table = jnp.zeros(bias_table.shape, jnp.float32)
    outputs = []
    for cell_slot in range(CELLS):
        table_row = bias_table[cell_ids[cell_slot]]
        cell_buckets = buckets[cell_slot]
        cell_grads = d_attended[cell_slot].reshape(total_rows, HEADS, HD)

        def step_block(loop_carry, block_index):
            key_sum, value_sum, table_sum = loop_carry
            row_first = (block_index * block_rows).astype(jnp.int32)
            query_blk = lax.dynamic_slice_in_dim(queries, row_first, block_rows, 0)
            grad_blk = lax.dynamic_slice_in_dim(cell_grads, row_first, block_rows, 0)
            key_blk = lax.dynamic_slice_in_dim(padded_keys, row_first, span_rows, 0)
            value_blk = lax.dynamic_slice_in_dim(padded_values, row_first, span_rows, 0)
            tile_first = row_first // TILE
            bucket_blk = lax.dynamic_slice_in_dim(cell_buckets, tile_first, tiles_block, 0)
            query_tiles = tile_first + jnp.arange(tiles_block, dtype=jnp.int32)
            bias_terms, inside, onehot = tile_bias(bucket_blk, table_row, query_tiles, row_first - half_band, span_rows, tile_total)
            scores, keep_mask = band_scores(query_blk, key_blk, bias_terms, inside, factor)
            row_top = lax.optimization_barrier(jnp.max(scores, axis=2))
            row_mass = lax.optimization_barrier(jnp.sum(jnp.where(keep_mask, jnp.exp(scores - row_top[:, :, None]), 0.0), axis=2))
            log_total = row_top + jnp.log(row_mass)
            chance = jnp.where(keep_mask, jnp.exp(scores - log_total[:, :, None]), 0.0)
            chance_b = chance.astype(jnp.bfloat16)
            attended_blk = jnp.einsum('qhk,khd->qhd', chance_b.astype(jnp.float32), value_blk.astype(jnp.float32)).astype(jnp.bfloat16)
            row_delta = lax.optimization_barrier(jnp.sum(grad_blk.astype(jnp.float32) * attended_blk.astype(jnp.float32), axis=2))
            grad_push = jnp.einsum('qhd,khd->qhk', grad_blk.astype(jnp.float32), value_blk.astype(jnp.float32))
            dscore = chance * (grad_push - row_delta[:, :, None])
            q_part = jnp.einsum('qhk,khd->qhd', dscore, key_blk.astype(jnp.float32), precision=lax.Precision.HIGHEST) * factor
            key_part = jnp.einsum('qhk,qhd->khd', dscore, query_blk.astype(jnp.float32), precision=lax.Precision.HIGHEST) * factor
            value_part = jnp.einsum('qhk,qhd->khd', chance_b.astype(jnp.float32), grad_blk.astype(jnp.float32))
            key_sum = lax.dynamic_update_slice_in_dim(key_sum, lax.dynamic_slice_in_dim(key_sum, row_first, span_rows, 0) + key_part, row_first, 0)
            value_sum = lax.dynamic_update_slice_in_dim(value_sum, lax.dynamic_slice_in_dim(value_sum, row_first, span_rows, 0) + value_part, row_first, 0)
            tile_sum = dscore.reshape(tiles_block, TILE, HEADS, span_rows).sum(axis=1)
            table_sum = table_sum + jnp.einsum('qhk,qkb->bh', tile_sum, onehot, precision=lax.Precision.HIGHEST)
            return ((key_sum, value_sum, table_sum), (attended_blk, q_part))
        start_carry = (jnp.zeros((padded_total, HEADS, HD), jnp.float32), jnp.zeros((padded_total, HEADS, HD), jnp.float32), jnp.zeros((bias_table.shape[1], HEADS), jnp.float32))
        final_carry, stacked = lax.scan(step_block, start_carry, jnp.arange(block_count, dtype=jnp.int32))
        key_grad = key_grad + final_carry[0][half_band:half_band + total_rows]
        value_grad = value_grad + final_carry[1][half_band:half_band + total_rows]
        grad_table = grad_table.at[cell_ids[cell_slot]].add(final_carry[2])
        outputs.append(stacked[0].reshape(total_rows, inner_width))
        query_grad = query_grad + stacked[1].reshape(total_rows, HEADS, HD)
    attended = jnp.stack(outputs, axis=0)
    grad_rows = jnp.concatenate([query_grad.reshape(total_rows, inner_width), key_grad.reshape(total_rows, inner_width), value_grad.reshape(total_rows, inner_width)], axis=1)
    grad_qkv = jnp.dot(features.astype(jnp.float32).T, grad_rows, precision=lax.Precision.HIGHEST, preferred_element_type=jnp.float32)
    return (attended, grad_qkv, grad_table)
```

```python
import math

import jax
import jax.numpy as jnp
from jax import lax
from jax.experimental import pallas as pl
from jax.experimental.pallas import tpu as pltpu
from jax.sharding import PartitionSpec as P

HEADS = 2
HD = 128
TILE = 128
BT = 16
NSEQ = 32
NWIN = 17
TPAD = 24
NEG = -1e30
FACTOR = 1.0 / math.sqrt(HD)
F32 = jnp.float32
BF16 = jnp.bfloat16

S_FEAT = 0
S_FCROSS = 7
S_DO = 8
S_BIAS = 11
S_KV = 14
S_Q = 17
S_WIN = 18
S_ATT = 26
S_TT = 29
S_DKV = 32
S_XKV = 40
S_XQ = 43
S_GC = 46
S_TC = 47
S_GY = 48
S_TY = 51
S_GZ = 54
S_TZ = 61
S_TX = 68
S_OY = 71
S_OC = 74
N_SEM = 75

WIN_OFFSETS = (-4, 4, -3, 3, -2, 2, -1, 1)


def dot_nn(a, b):
    return lax.dot_general(a, b, (((1,), (0,)), ((), ())), preferred_element_type=F32)


def dot_nt(a, b):
    return lax.dot_general(a, b, (((1,), (1,)), ((), ())), preferred_element_type=F32)


def dot_tn(a, b):
    return lax.dot_general(a, b, (((0,), (0,)), ((), ())), preferred_element_type=F32)


def kernel(
    feat_ref, w_hbm, bias_ref, oht_ref, hit_ref, dout_ref,
    att_out, grad_out, table_out,
    w_ref, fbuf, fcross, dot_src, dot_buf, bias_buf, proj_kv, proj_q, q_buf, kvw,
    e0_buf, o_buf, m_buf, l_buf, d_buf, w_buf, dof_buf,
    att_src, att_buf, tt_src, tt_buf, dkvw, dkv_in, dkv_x, dq_x, d3,
    g_src, g_core, g_c, g_y, g_zs, g_z, g_oy, g_oc,
    t_c, t_y, t_z, t_x, w_sem, send_sem, recv_sem,
):
    cell = lax.axis_index("cell")
    seq = lax.axis_index("seq")
    zh = cell // 4
    x = cell % 4
    z_lo = seq // 8
    y = (seq // 2) % 4
    core = seq % 2
    zi = zh * 4 + z_lo
    head = x % 2
    half = x // 2

    def at_x(k):
        return (zh * 4 + (x + k) % 4, seq)

    def at_cross(k):
        return ((1 - zh) * 4 + (x + k) % 4, seq)

    def at_seq(o):
        return (cell, (seq + o + NSEQ) % NSEQ)

    def at_y(k):
        return (cell, z_lo * 8 + ((y + k) % 4) * 2 + core)

    def at_z(k):
        there = (zi + k) % 8
        return ((there // 4) * 4 + x, (there % 4) * 8 + y * 2 + core)

    sibling = (cell, seq + 1 - 2 * core)

    w_copy = pltpu.make_async_copy(w_hbm, w_ref, w_sem)
    w_copy.start()

    barrier = pltpu.get_barrier_semaphore()
    greet = [at_cross(k) for k in range(4)] + [at_x(k) for k in (1, 2, 3)]
    greet += [at_seq(o) for o in WIN_OFFSETS]
    greet += [at_y(k) for k in (1, 2, 3)] + [at_z(k) for k in range(1, 8)]
    for peer in greet:
        pl.semaphore_signal(barrier, inc=1, device_id=peer, device_id_type=pl.DeviceIdType.MESH)

    sends = []

    def remote(src, dst, slot, peer):
        copy = pltpu.make_async_remote_copy(
            src_ref=src,
            dst_ref=dst,
            send_sem=send_sem.at[slot],
            recv_sem=recv_sem.at[slot],
            device_id=peer,
            device_id_type=pl.DeviceIdType.MESH,
        )
        copy.start()
        sends.append(copy)
        return copy

    for piece in range(4):
        r, h = piece // 2, piece % 2
        block = dout_ref[128 * r : 128 * r + 128, 128 * h : 128 * h + 128]
        dot_src[piece] = block.astype(F32).T.astype(BF16)

    pl.semaphore_wait(barrier, len(greet))

    feat_in = []
    for k in range(4):
        there = (x + k) % 4
        feat_in.append(
            remote(feat_ref.at[pl.ds(64 * there, 64)], fbuf.at[cell], S_FEAT + k, at_cross(k))
        )
    for k in (1, 2, 3):
        there = (x + k) % 4
        feat_in.append(
            remote(feat_ref.at[pl.ds(64 * there, 64)], fbuf.at[cell], S_FEAT + 3 + k, at_x(k))
        )
    do_in = []
    bias_in = []
    for k in (1, 2, 3):
        there = (x + k) % 4
        do_in.append(remote(dot_src.at[there], dot_buf.at[x], S_DO + k - 1, at_x(k)))
        bias_in.append(remote(bias_ref.at[there], bias_buf.at[x], S_BIAS + k - 1, at_x(k)))
    cross_in = remote(feat_ref, fcross, S_FCROSS, at_cross(0))

    dot_buf[x] = dot_src[x]
    bias_buf[x] = bias_ref[x]
    fbuf[cell] = feat_ref[pl.ds(64 * x, 64), :]
    w_copy.wait()
    for copy in feat_in:
        copy.wait_recv()

    proj = jnp.zeros((64, 768), F32)
    for c in range(8):
        proj = proj + dot_nn(fbuf[c], w_ref[192 * c : 192 * c + 192, :])
    projected = proj.astype(BF16)
    for h in range(2):
        proj_q[h] = projected[:, 128 * h : 128 * h + 128]
        proj_kv[h, :, 0:128] = projected[:, 256 + 128 * h : 384 + 128 * h]
        proj_kv[h, :, 128:256] = projected[:, 512 + 128 * h : 640 + 128 * h]

    my_tile = 8 + x // 2
    my_rows = pl.ds(64 * (x % 2), 64)
    kv_in = []
    for k in (1, 2, 3):
        there = (x + k) % 4
        kv_in.append(
            remote(proj_kv.at[there % 2], kvw.at[my_tile, my_rows], S_KV + k - 1, at_x(k))
        )
    mate = (zh * 4 + x + 1 - 2 * (x % 2), seq)
    q_in = remote(proj_q.at[1 - head], q_buf.at[my_rows], S_Q, mate)
    kvw[my_tile, my_rows] = proj_kv[head]
    q_buf[my_rows] = proj_q[head]
    for copy in kv_in:
        copy.wait_recv()

    win_in = {}
    for n, o in enumerate(WIN_OFFSETS):
        count = 1 if o == -4 else 2
        win_in[4 - o] = remote(
            kvw.at[pl.ds(8, count)], kvw.at[pl.ds(8 - 2 * o, count)], S_WIN + n, at_seq(o)
        )
    q_in.wait_recv()
    for copy in do_in + bias_in:
        copy.wait_recv()

    q_tile = q_buf[...]
    for c in range(4):
        dof_buf[c] = dot_buf[c].astype(F32)
    m_buf[...] = jnp.zeros((TPAD, 128), F32)
    l_buf[...] = jnp.zeros((TPAD, 128), F32)
    d_buf[...] = jnp.zeros((4, TPAD, 128), F32)

    def forward_tile(t):
        keys = kvw[t, :, 0:128]
        values = kvw[t, :, 128:256]
        s = dot_nt(keys, q_tile) * FACTOR
        top = jnp.max(s, axis=0, keepdims=True)
        e0 = jnp.exp(s - top)
        m_buf[t : t + 1, :] = top
        l_buf[t : t + 1, :] = jnp.sum(e0, axis=0, keepdims=True)
        e0b = e0.astype(BF16)
        e0_buf[t] = e0b
        o_t = dot_tn(values, e0b)
        o_buf[t] = o_t
        for c in range(4):
            d_buf[c, t : t + 1, :] = jnp.sum(dof_buf[c] * o_t, axis=0, keepdims=True)

    for slot in (4, 3, 5, 2, 6, 1, 7, 0, 8):
        if slot != 4:
            win_in[slot].wait_recv()
        forward_tile(2 * slot)
        if slot != 8:
            forward_tile(2 * slot + 1)

    m_all = m_buf[...]
    l_all = l_buf[...]
    big = jnp.zeros((TPAD, 128), F32)
    att_in = []
    tt_in = []
    for c in range(4):
        z = m_all + bias_buf[c]
        top = jnp.max(z, axis=0, keepdims=True)
        ex = jnp.exp(z - top)
        mass = jnp.sum(ex * l_all, axis=0, keepdims=True)
        w_c = ex / mass
        w_buf[c] = w_c
        acc = jnp.zeros((128, 128), F32)
        for t in range(NWIN):
            acc = acc + w_c[t : t + 1, :] * o_buf[t]
        accb = acc.astype(BF16)
        att_src[c] = acc.T.astype(BF16)
        delta = jnp.sum(dof_buf[c] * accb.astype(F32), axis=0, keepdims=True)
        big = big + w_c * delta
        tt_src[c] = w_c * (d_buf[c] - delta * l_all)
    for k in (1, 2, 3):
        there = (x + k) % 4
        att_in.append(remote(att_src.at[there], att_buf.at[x], S_ATT + k - 1, at_x(k)))
        tt_in.append(remote(tt_src.at[there], tt_buf.at[x], S_TT + k - 1, at_x(k)))
    att_buf[x] = att_src[x]
    tt_buf[x] = tt_src[x]

    dq_acc = jnp.zeros((128, 128), F32)
    dkv_get = {}
    for slot in (0, 8, 1, 7, 2, 6, 3, 5, 4):
        for t in (2 * slot, 2 * slot + 1):
            if t >= NWIN:
                continue
            g_t = w_buf[0, t : t + 1, :] * dof_buf[0]
            for c in (1, 2, 3):
                g_t = g_t + w_buf[c, t : t + 1, :] * dof_buf[c]
            gb = g_t.astype(BF16)
            e0b = e0_buf[t]
            dp = dot_nn(kvw[t, :, 128:256], gb)
            ds = (e0b.astype(F32) * (dp - big[t : t + 1, :])).astype(BF16)
            dkvw[t, :, 0:128] = (dot_nn(ds, q_tile) * FACTOR).astype(BF16)
            dkvw[t, :, 128:256] = dot_nt(e0b, gb).astype(BF16)
            dq_acc = dq_acc + dot_tn(ds, kvw[t, :, 0:128])
        o = slot - 4
        if o != 0:
            n = WIN_OFFSETS.index(o)
            count = 1 if o == 4 else 2
            dkv_get[4 - o] = remote(
                dkvw.at[pl.ds(2 * slot, count)],
                dkv_in.at[pl.ds(2 * (4 - o), count)],
                S_DKV + n,
                at_seq(o),
            )
    dq_x[x] = (dq_acc * FACTOR).astype(BF16)
    xq_in = [remote(dq_x.at[x], dq_x.at[x], S_XQ + k - 1, at_x(k)) for k in (1, 2, 3)]

    for copy in tt_in:
        copy.wait_recv()
    ones = jnp.ones((8, 128), F32)
    row = jnp.zeros((8, 128), F32)
    for piece in range(4):
        sums = lax.dot_general(
            ones, tt_buf[piece], (((1,), (1,)), ((), ())),
            precision=lax.Precision.HIGHEST, preferred_element_type=F32,
        )
        row = row + lax.dot_general(
            sums, oht_ref[piece], (((1,), (0,)), ((), ())),
            precision=lax.Precision.HIGHEST, preferred_element_type=F32,
        )
    t_c[core] = hit_ref[...] * row[0:1, :]
    tc_in = remote(t_c.at[core], t_c.at[core], S_TC, sibling)

    for copy in att_in:
        copy.wait_recv()
    for piece in range(4):
        r, h = piece // 2, piece % 2
        att_out[128 * r : 128 * r + 128, 128 * h : 128 * h + 128] = att_buf[piece]

    for slot in (4, 3, 5, 2, 6, 1, 7, 0, 8):
        if slot != 4:
            dkv_get[slot].wait_recv()
    for t in range(2):
        acc = dkvw[8 + t].astype(F32)
        for slot in (3, 5, 2, 6, 1, 7, 0, 8):
            if slot == 0 and t == 1:
                continue
            acc = acc + dkv_in[2 * slot + t].astype(F32)
        dkv_x[x, t] = acc.astype(BF16)
    xkv_in = [remote(dkv_x.at[x], dkv_x.at[x], S_XKV + k - 1, at_x(k)) for k in (1, 2, 3)]

    tc_in.wait_recv()
    t_y[y] = t_c[0] + t_c[1]
    ty_in = [remote(t_y.at[y], t_y.at[y], S_TY + k - 1, at_y(k)) for k in (1, 2, 3)]

    for copy in xq_in + xkv_in:
        copy.wait_recv()
    for t in range(2):
        for h in range(2):
            rows = slice(128 * t, 128 * t + 128)
            d3[rows, 128 * h : 128 * h + 128] = dq_x[2 * t + h]
            both = dkv_x[h, t].astype(F32) + dkv_x[2 + h, t].astype(F32)
            bothb = both.astype(BF16)
            d3[rows, 256 + 128 * h : 384 + 128 * h] = bothb[:, 0:128]
            d3[rows, 512 + 128 * h : 640 + 128 * h] = bothb[:, 128:256]

    cross_in.wait_recv()
    d_all = d3[...]
    own = dot_tn(feat_ref[...], d_all).astype(BF16)
    other = dot_tn(fcross[...], d_all).astype(BF16)
    for k in range(2):
        g_src[k, zh] = own[:, 384 * k : 384 * k + 384]
        g_src[k, 1 - zh] = other[:, 384 * k : 384 * k + 384]
    gc_in = remote(g_src.at[1 - core], g_core, S_GC, sibling)

    for copy in ty_in:
        copy.wait_recv()
    t_z[zi] = (t_y[0] + t_y[1]) + (t_y[2] + t_y[3])
    tz_in = [remote(t_z.at[zi], t_z.at[zi], S_TZ + k - 1, at_z(k)) for k in range(1, 8)]

    gc_in.wait_recv()
    g_c[...] = (g_src[core].astype(F32) + g_core[...].astype(F32)).astype(BF16)
    gy_in = []
    for k in (1, 2, 3):
        there = (y + k) % 4
        gy_in.append(
            remote(g_c.at[:, pl.ds(48 * there, 48)], g_y.at[y], S_GY + k - 1, at_y(k))
        )
    g_y[y] = g_c[:, pl.ds(48 * y, 48), :]

    for copy in tz_in:
        copy.wait_recv()
    total = t_z[0]
    for k in range(1, 8):
        total = total + t_z[k]
    t_x[x] = total
    tx_in = [remote(t_x.at[x], t_x.at[x], S_TX + k - 1, at_x(k)) for k in (1, 2, 3)]

    for copy in gy_in:
        copy.wait_recv()
    piece = g_y[0].astype(F32)
    for k in (1, 2, 3):
        piece = piece + g_y[k].astype(F32)
    g_zs[...] = piece.astype(BF16)
    gz_in = []
    for k in (4, 3, 5, 2, 6, 1, 7):
        there = (zi + k) % 8
        gz_in.append(remote(g_zs.at[there // 4], g_z.at[zi], S_GZ + k - 1, at_z(k)))
    g_z[zi] = g_zs[zh]

    for copy in tx_in:
        copy.wait_recv()
    table_out[...] = (t_x[0] + t_x[1]) + (t_x[2] + t_x[3])

    for copy in gz_in:
        copy.wait_recv()
    piece = g_z[0].astype(F32)
    for k in range(1, 8):
        piece = piece + g_z[k].astype(F32)
    g_oy[y] = piece.astype(BF16)
    oy_in = [remote(g_oy.at[y], g_oy.at[y], S_OY + k - 1, at_y(k)) for k in (1, 2, 3)]
    for copy in oy_in:
        copy.wait_recv()
    oc_in = remote(g_oy, g_oc, S_OC, sibling)
    oc_in.wait_recv()
    first = core == 0
    for k in range(4):
        mine = g_oy[k].astype(F32)
        theirs = g_oc[k].astype(F32)
        grad_out[48 * k : 48 * k + 48, 0:384] = jnp.where(first, mine, theirs)
        grad_out[48 * k : 48 * k + 48, 384:768] = jnp.where(first, theirs, mine)
    for copy in sends:
        copy.wait_send()


def local(features, w_qkv, buckets, cell_ids, bias_table, d_attended):
    seq = lax.axis_index("seq")
    types, levels, _ = bias_table.shape
    type_hit = jnp.arange(types, dtype=jnp.int32) == cell_ids[0]
    table_row = jnp.sum(jnp.where(type_hit[:, None, None], bias_table, 0.0), axis=0)
    tile_at = jnp.arange(TPAD, dtype=jnp.int32)
    padded = jnp.stack(
        [jnp.pad(buckets[0, r], (r, TPAD - BT - r), constant_values=-1) for r in range(2)]
    )
    global_tile = 2 * seq - 8 + tile_at
    in_range = (global_tile >= 0) & (global_tile < 2 * NSEQ)
    onehot = padded[:, :, None] == jnp.arange(levels, dtype=jnp.int32)
    bias = jnp.sum(jnp.where(onehot[:, None], table_row.T[None, :, None, :], 0.0), axis=3)
    valid = (padded >= 0) & in_range[None, :]
    bias = jnp.where(valid[:, None, :], bias, NEG)
    bias_in = jnp.broadcast_to(bias.reshape(4, TPAD, 1), (4, TPAD, 128))
    lane = jnp.arange(128, dtype=jnp.int32)
    head_at = jnp.arange(2, dtype=jnp.int32)
    wanted = head_at[None, :, None] * levels + padded[:, None, :]
    oht = ((wanted[..., None] == lane) & (padded >= 0)[:, None, :, None]).astype(F32)
    oht = oht.reshape(4, TPAD, 128)
    hit = jnp.broadcast_to(type_hit[:, None], (types, 128)).astype(F32)

    vmem = pl.BlockSpec(memory_space=pltpu.VMEM)
    hbm = pl.BlockSpec(memory_space=pl.ANY)
    scratch = [
        pltpu.VMEM((1536, 768), BF16),
        pltpu.VMEM((8, 64, 192), BF16),
        pltpu.VMEM((256, 192), BF16),
        pltpu.VMEM((4, 128, 128), BF16),
        pltpu.VMEM((4, 128, 128), BF16),
        pltpu.VMEM((4, TPAD, 128), F32),
        pltpu.VMEM((2, 64, 256), BF16),
        pltpu.VMEM((2, 64, 128), BF16),
        pltpu.VMEM((128, 128), BF16),
        pltpu.VMEM((18, 128, 256), BF16),
        pltpu.VMEM((NWIN, 128, 128), BF16),
        pltpu.VMEM((NWIN, 128, 128), F32),
        pltpu.VMEM((TPAD, 128), F32),
        pltpu.VMEM((TPAD, 128), F32),
        pltpu.VMEM((4, TPAD, 128), F32),
        pltpu.VMEM((4, TPAD, 128), F32),
        pltpu.VMEM((4, 128, 128), F32),
        pltpu.VMEM((4, 128, 128), BF16),
        pltpu.VMEM((4, 128, 128), BF16),
        pltpu.VMEM((4, TPAD, 128), F32),
        pltpu.VMEM((4, TPAD, 128), F32),
        pltpu.VMEM((18, 128, 256), BF16),
        pltpu.VMEM((18, 128, 256), BF16),
        pltpu.VMEM((4, 2, 128, 256), BF16),
        pltpu.VMEM((4, 128, 128), BF16),
        pltpu.VMEM((256, 768), BF16),
        pltpu.VMEM((2, 2, 192, 384), BF16),
        pltpu.VMEM((2, 192, 384), BF16),
        pltpu.VMEM((2, 192, 384), BF16),
        pltpu.VMEM((4, 2, 48, 384), BF16),
        pltpu.VMEM((2, 48, 384), BF16),
        pltpu.VMEM((8, 48, 384), BF16),
        pltpu.VMEM((4, 48, 384), BF16),
        pltpu.VMEM((4, 48, 384), BF16),
        pltpu.VMEM((2, 32, 128), F32),
        pltpu.VMEM((4, 32, 128), F32),
        pltpu.VMEM((8, 32, 128), F32),
        pltpu.VMEM((4, 32, 128), F32),
        pltpu.SemaphoreType.DMA,
        pltpu.SemaphoreType.DMA((N_SEM,)),
        pltpu.SemaphoreType.DMA((N_SEM,)),
    ]
    att, grad, table = pl.pallas_call(
        kernel,
        out_shape=(
            jax.ShapeDtypeStruct((256, 256), BF16),
            jax.ShapeDtypeStruct((192, 768), F32),
            jax.ShapeDtypeStruct((types, 128), F32),
        ),
        in_specs=[vmem, hbm, vmem, vmem, vmem, vmem],
        out_specs=(vmem, vmem, vmem),
        scratch_shapes=scratch,
        compiler_params=pltpu.CompilerParams(collective_id=0, has_side_effects=True),
    )(features, w_qkv, bias_in, oht, hit, d_attended[0])
    grad_table = table[:, : HEADS * levels].reshape(types, HEADS, levels).transpose(0, 2, 1)
    return (att[None], grad, grad_table)


def solution(mesh):
    in_specs = (
        P("seq", "cell"),
        P(),
        P("cell", "seq", None),
        P("cell"),
        P(),
        P("cell", "seq", None),
    )
    out_specs = (P("cell", "seq", None), P("cell", None), P())
    return jax.shard_map(local, mesh=mesh, in_specs=in_specs, out_specs=out_specs, check_vma=False)
```

```python
import math

import jax
import jax.numpy as jnp
from jax import lax
from jax.experimental import pallas as pl
from jax.experimental.pallas import tpu as pltpu
from jax.sharding import PartitionSpec as P

HEADS = 2
HD = 128
TILE = 128
BT = 16
NSEQ = 32
NWIN = 17
TPAD = 24
NEG = -1e30
FACTOR = 1.0 / math.sqrt(HD)
F32 = jnp.float32
BF16 = jnp.bfloat16

S_FEAT = 0
S_FCROSS = 7
S_DO = 8
S_BIAS = 11
S_KV = 14
S_Q = 17
S_NEAR = 18
S_FAR = 22
S_ATT = 26
S_TT = 29
S_DKV = 32
S_XKV = 40
S_XQ = 43
S_GC = 46
S_TC = 47
S_GY = 48
S_TY = 51
S_GZ = 54
S_TZ = 61
S_TX = 68
S_OY = 71
S_OC = 74
S_SIB = 75
S_GC2 = 83
N_SEM = 84

WIN_OFFSETS = (-4, 4, -3, 3, -2, 2, -1, 1)


def dot_nn(a, b):
    return lax.dot_general(a, b, (((1,), (0,)), ((), ())), preferred_element_type=F32)


def dot_nt(a, b):
    return lax.dot_general(a, b, (((1,), (1,)), ((), ())), preferred_element_type=F32)


def dot_tn(a, b):
    return lax.dot_general(a, b, (((0,), (0,)), ((), ())), preferred_element_type=F32)


def kernel(
    ft_hbm, w_hbm, buckets_ref, ids_ref, tbl_hbm, dout_hbm,
    att_out, grad_out, table_out,
    ft_ref, feat_ref, dout_ref, tbl_ref, row_buf, oh_buf, bias_ref, w_ref, fbuf, fcross, dot_src, dot_buf, bias_buf, proj_kv, proj_q, q_buf, kvw,
    e0_buf, o_buf, m_buf, l_buf, d_buf, w_buf, dof_buf,
    att_src, att_buf, tt_src, tt_buf, dkvw, dkv_in, dkv_x, dq_x, d3,
    g_src, g_mine, g_core, g_c, g_y, g_zs, g_z, g_oy, g_oc,
    t_c, t_y, t_z, t_x, in_sem, send_sem, recv_sem,
):
    cell = lax.axis_index("cell")
    seq = lax.axis_index("seq")
    zh = cell // 4
    x = cell % 4
    z_lo = seq // 8
    y = (seq // 2) % 4
    core = seq % 2
    zi = zh * 4 + z_lo
    head = x % 2
    half = x // 2

    def at_x(k):
        return (zh * 4 + (x + k) % 4, seq)

    def at_cross(k):
        return ((1 - zh) * 4 + (x + k) % 4, seq)

    def at_seq(o):
        return (cell, (seq + o + NSEQ) % NSEQ)

    def at_y(k):
        return (cell, z_lo * 8 + ((y + k) % 4) * 2 + core)

    def at_z(k):
        there = (zi + k) % 8
        return ((there // 4) * 4 + x, (there % 4) * 8 + y * 2 + core)

    sibling = (cell, seq + 1 - 2 * core)

    ft_copy = pltpu.make_async_copy(ft_hbm, ft_ref, in_sem.at[0])
    ft_copy.start()
    barrier = pltpu.get_barrier_semaphore()
    greet = [at_cross(k) for k in range(4)] + [at_x(k) for k in (1, 2, 3)]
    greet += [at_seq(o) for o in WIN_OFFSETS] + [sibling]
    greet += [at_y(k) for k in (1, 2, 3)] + [at_z(k) for k in range(1, 8)]
    for peer in greet:
        pl.semaphore_signal(barrier, inc=1, device_id=peer, device_id_type=pl.DeviceIdType.MESH)

    sends = []

    def remote(src, dst, slot, peer):
        copy = pltpu.make_async_remote_copy(
            src_ref=src,
            dst_ref=dst,
            send_sem=send_sem.at[slot],
            recv_sem=recv_sem.at[slot],
            device_id=peer,
            device_id_type=pl.DeviceIdType.MESH,
        )
        copy.start()
        sends.append(copy)
        return copy

    dout_copy = pltpu.make_async_copy(dout_hbm.at[0], dout_ref, in_sem.at[1])
    dout_copy.start()
    tbl_copy = pltpu.make_async_copy(tbl_hbm, tbl_ref, in_sem.at[2])
    tbl_copy.start()
    w_copy = pltpu.make_async_copy(w_hbm, w_ref, in_sem.at[3])
    w_copy.start()
    ft_copy.wait()
    feat_ref[...] = ft_ref[...].astype(F32).T.astype(BF16)
    pl.semaphore_wait(barrier, len(greet))

    feat_in = []
    for k in range(4):
        there = (x + k) % 4
        feat_in.append(
            remote(feat_ref.at[pl.ds(64 * there, 64)], fbuf.at[cell], S_FEAT + k, at_cross(k))
        )
    for k in (1, 2, 3):
        there = (x + k) % 4
        feat_in.append(
            remote(feat_ref.at[pl.ds(64 * there, 64)], fbuf.at[cell], S_FEAT + 3 + k, at_x(k))
        )
    dout_copy.wait()
    for piece in range(4):
        r, h = piece // 2, piece % 2
        block = dout_ref[128 * r : 128 * r + 128, 128 * h : 128 * h + 128]
        dot_src[piece] = block.astype(F32).T.astype(BF16)
    lane = lax.broadcasted_iota(jnp.int32, (1, 128), 1)
    oh_buf[...] = jnp.zeros((2, TPAD, 128), F32)
    row_buf[...] = jnp.zeros((8, 128), F32)
    for r in range(2):
        for o in range(BT):
            oh_buf[r, r + o : r + o + 1, :] = (lane == buckets_ref[0, r, o]).astype(F32)
    tbl_copy.wait()
    hit = (lax.broadcasted_iota(jnp.int32, (32, 128), 0) == ids_ref[0]).astype(F32)
    tile_at = lax.broadcasted_iota(jnp.int32, (TPAD, 128), 0)
    global_tile = 2 * seq - 8 + tile_at
    in_range = (global_tile >= 0) & (global_tile < 2 * NSEQ)
    for h in range(2):
        row_buf[h : h + 1, 0:32] = jnp.sum(
            jnp.where(hit[:, 0:32] > 0.0, tbl_ref[:, h, :], 0.0), axis=0, keepdims=True
        )
        for r in range(2):
            level = jnp.sum(oh_buf[r] * row_buf[h : h + 1, :], axis=1, keepdims=True)
            valid = in_range & (tile_at >= r) & (tile_at < r + BT)
            bias_ref[2 * r + h] = jnp.where(valid, jnp.broadcast_to(level, (TPAD, 128)), NEG)

    do_in = []
    bias_in = []
    for k in (1, 2, 3):
        there = (x + k) % 4
        do_in.append(remote(dot_src.at[there], dot_buf.at[x], S_DO + k - 1, at_x(k)))
        bias_in.append(remote(bias_ref.at[there], bias_buf.at[x], S_BIAS + k - 1, at_x(k)))
    cross_in = remote(ft_ref, fcross, S_FCROSS, at_cross(0))

    dot_buf[x] = dot_src[x]
    bias_buf[x] = bias_ref[x]
    fbuf[cell] = feat_ref[pl.ds(64 * x, 64), :]
    w_copy.wait()
    for copy in feat_in:
        copy.wait_recv()

    proj = jnp.zeros((64, 768), F32)
    for c in range(8):
        proj = proj + dot_nn(fbuf[c], w_ref[192 * c : 192 * c + 192, :])
    projected = proj.astype(BF16)
    for h in range(2):
        proj_q[h] = projected[:, 128 * h : 128 * h + 128]
        proj_kv[h, :, 0:128] = projected[:, 256 + 128 * h : 384 + 128 * h]
        proj_kv[h, :, 128:256] = projected[:, 512 + 128 * h : 640 + 128 * h]

    my_tile = 8 + x // 2
    my_rows = pl.ds(64 * (x % 2), 64)
    kv_in = []
    for k in (1, 2, 3):
        there = (x + k) % 4
        kv_in.append(
            remote(proj_kv.at[there % 2], kvw.at[my_tile, my_rows], S_KV + k - 1, at_x(k))
        )
    mate = (zh * 4 + x + 1 - 2 * (x % 2), seq)
    q_in = remote(proj_q.at[1 - head], q_buf.at[my_rows], S_Q, mate)
    kvw[my_tile, my_rows] = proj_kv[head]
    q_buf[my_rows] = proj_q[head]
    for copy in kv_in:
        copy.wait_recv()

    def relay(src_tile, dst_tile, slot):
        return remote(kvw.at[src_tile], kvw.at[dst_tile], slot, sibling)

    near = {}
    far = {}
    mate_in = {}
    pairs = [(t, d) for t in range(2) for d in (-1, 1)]
    for n, (t, d) in enumerate(pairs):
        near[-d, t] = remote(kvw.at[8 + t], kvw.at[8 - 4 * d + t], S_NEAR + n, at_seq(2 * d))
    for t in range(2):
        mate_in[0, t] = relay(8 + t, 6 + 4 * core + t, S_SIB + t)

    def pass_on(t):
        for d in (-1, 1):
            near[d, t].wait_recv()
            here = 8 + 4 * d + t
            n = pairs.index((t, d))
            far[2 * d, t] = remote(
                kvw.at[here], kvw.at[8 + 8 * d + t], S_FAR + n, at_seq(-2 * d)
            )
            mate_in[d, t] = relay(here, 6 + 4 * d + 4 * core + t, S_SIB + 2 + n)

    def pass_far(t):
        for d in (-2, 2):
            far[d, t].wait_recv()
        mate_in[2, t] = relay(16 - 16 * core + t, 14 - 12 * core + t, S_SIB + 6 + t)

    q_in.wait_recv()
    for copy in do_in + bias_in:
        copy.wait_recv()

    q_tile = q_buf[...]
    for c in range(4):
        dof_buf[c] = dot_buf[c].astype(F32)
    m_buf[...] = jnp.zeros((TPAD, 128), F32)
    l_buf[...] = jnp.zeros((TPAD, 128), F32)
    d_buf[...] = jnp.zeros((4, TPAD, 128), F32)

    def forward_tile(t):
        keys = kvw[t, :, 0:128]
        values = kvw[t, :, 128:256]
        s = dot_nt(keys, q_tile) * FACTOR
        top = jnp.max(s, axis=0, keepdims=True)
        e0 = jnp.exp(s - top)
        m_buf[pl.ds(t, 1), :] = top
        l_buf[pl.ds(t, 1), :] = jnp.sum(e0, axis=0, keepdims=True)
        e0b = e0.astype(BF16)
        e0_buf[t] = e0b
        o_t = dot_tn(values, e0b)
        o_buf[t] = o_t
        for c in range(4):
            d_buf[c, pl.ds(t, 1), :] = jnp.sum(dof_buf[c] * o_t, axis=0, keepdims=True)

    forward_tile(8)
    pass_on(0)
    forward_tile(9)
    pass_on(1)
    for t in range(2):
        mate_in[0, t].wait_recv()
        forward_tile(10 - 4 * core + t)
    for t in range(2):
        for d in (-1, 1):
            forward_tile(8 + 4 * d + t)
    pass_far(0)
    for t in range(2):
        for d in (-1, 1):
            mate_in[d, t].wait_recv()
            forward_tile(10 + 4 * d - 4 * core + t)
    pass_far(1)
    forward_tile(0)
    forward_tile(1)
    forward_tile(16)
    for t in range(2):
        mate_in[2, t].wait_recv()
        forward_tile(2 + 12 * core + t)

    m_all = m_buf[...]
    l_all = l_buf[...]
    big = jnp.zeros((TPAD, 128), F32)
    att_in = []
    tt_in = []
    for c in range(4):
        z = m_all + bias_buf[c]
        top = jnp.max(z, axis=0, keepdims=True)
        ex = jnp.exp(z - top)
        mass = jnp.sum(ex * l_all, axis=0, keepdims=True)
        w_c = ex / mass
        w_buf[c] = w_c
        acc = jnp.zeros((128, 128), F32)
        for t in range(NWIN):
            acc = acc + w_c[t : t + 1, :] * o_buf[t]
        accb = acc.astype(BF16)
        att_src[c] = acc.T.astype(BF16)
        delta = jnp.sum(dof_buf[c] * accb.astype(F32), axis=0, keepdims=True)
        big = big + w_c * delta
        tt_src[c] = w_c * (d_buf[c] - delta * l_all)
    for k in (1, 2, 3):
        there = (x + k) % 4
        att_in.append(remote(att_src.at[there], att_buf.at[x], S_ATT + k - 1, at_x(k)))
        tt_in.append(remote(tt_src.at[there], tt_buf.at[x], S_TT + k - 1, at_x(k)))
    att_buf[x] = att_src[x]
    tt_buf[x] = tt_src[x]

    dq_acc = jnp.zeros((128, 128), F32)
    dkv_get = {}
    for slot in (0, 8, 1, 7, 2, 6, 3, 5, 4):
        for t in (2 * slot, 2 * slot + 1):
            if t >= NWIN:
                continue
            g_t = w_buf[0, t : t + 1, :] * dof_buf[0]
            for c in (1, 2, 3):
                g_t = g_t + w_buf[c, t : t + 1, :] * dof_buf[c]
            gb = g_t.astype(BF16)
            e0b = e0_buf[t]
            dp = dot_nn(kvw[t, :, 128:256], gb)
            ds = (e0b.astype(F32) * (dp - big[t : t + 1, :])).astype(BF16)
            dkvw[t, :, 0:128] = (dot_nn(ds, q_tile) * FACTOR).astype(BF16)
            dkvw[t, :, 128:256] = dot_nt(e0b, gb).astype(BF16)
            dq_acc = dq_acc + dot_tn(ds, kvw[t, :, 0:128])
        o = slot - 4
        if o != 0:
            n = WIN_OFFSETS.index(o)
            count = 1 if o == 4 else 2
            dkv_get[4 - o] = remote(
                dkvw.at[pl.ds(2 * slot, count)],
                dkv_in.at[pl.ds(2 * (4 - o), count)],
                S_DKV + n,
                at_seq(o),
            )
    dq_x[x] = (dq_acc * FACTOR).astype(BF16)
    xq_in = [remote(dq_x.at[x], dq_x.at[x], S_XQ + k - 1, at_x(k)) for k in (1, 2, 3)]

    for copy in tt_in:
        copy.wait_recv()
    ones = jnp.ones((8, 128), F32)
    rows = []
    for h in range(2):
        row = jnp.zeros((8, 128), F32)
        for r in range(2):
            sums = lax.dot_general(
                ones, tt_buf[2 * r + h], (((1,), (1,)), ((), ())),
                precision=lax.Precision.HIGHEST, preferred_element_type=F32,
            )
            row = row + lax.dot_general(
                sums, oh_buf[r], (((1,), (0,)), ((), ())),
                precision=lax.Precision.HIGHEST, preferred_element_type=F32,
            )
        rows.append(row)
    both_heads = rows[0] + pltpu.roll(rows[1], 32, axis=1)
    t_c[core] = hit * both_heads[0:1, :]
    tc_in = remote(t_c.at[core], t_c.at[core], S_TC, sibling)

    for copy in att_in:
        copy.wait_recv()
    for piece in range(4):
        r, h = piece // 2, piece % 2
        att_out[128 * r : 128 * r + 128, 128 * h : 128 * h + 128] = att_buf[piece]

    for slot in (4, 3, 5, 2, 6, 1, 7, 0, 8):
        if slot != 4:
            dkv_get[slot].wait_recv()
    for t in range(2):
        acc = dkvw[8 + t].astype(F32)
        for slot in (3, 5, 2, 6, 1, 7, 0, 8):
            if slot == 0 and t == 1:
                continue
            acc = acc + dkv_in[2 * slot + t].astype(F32)
        dkv_x[x, t] = acc.astype(BF16)
    xkv_in = [remote(dkv_x.at[x], dkv_x.at[x], S_XKV + k - 1, at_x(k)) for k in (1, 2, 3)]

    tc_in.wait_recv()
    t_y[y] = t_c[0] + t_c[1]
    ty_in = [remote(t_y.at[y], t_y.at[y], S_TY + k - 1, at_y(k)) for k in (1, 2, 3)]

    for copy in xq_in + xkv_in:
        copy.wait_recv()
    for t in range(2):
        at_rows = slice(128 * t, 128 * t + 128)
        for h in range(2):
            d3[0, at_rows, 128 * h : 128 * h + 128] = dq_x[2 * t + h]
            both = dkv_x[h, t].astype(F32) + dkv_x[2 + h, t].astype(F32)
            bothb = both.astype(BF16)
            d3[h, at_rows, 256 - 256 * h : 384 - 256 * h] = bothb[:, 0:128]
            d3[1, at_rows, 128 + 128 * h : 256 + 128 * h] = bothb[:, 128:256]

    cross_in.wait_recv()
    theirs = d3[1 - core]
    g_src[zh] = dot_nn(ft_ref[...], theirs).astype(BF16)
    gc_in = [remote(g_src.at[zh], g_core.at[zh], S_GC, sibling)]
    g_src[1 - zh] = dot_nn(fcross[...], theirs).astype(BF16)
    gc_in.append(remote(g_src.at[1 - zh], g_core.at[1 - zh], S_GC2, sibling))
    mine = d3[core]
    g_mine[zh] = dot_nn(ft_ref[...], mine)
    g_mine[1 - zh] = dot_nn(fcross[...], mine)

    for copy in ty_in:
        copy.wait_recv()
    t_z[zi] = (t_y[0] + t_y[1]) + (t_y[2] + t_y[3])
    tz_in = [remote(t_z.at[zi], t_z.at[zi], S_TZ + k - 1, at_z(k)) for k in range(1, 8)]

    for copy in gc_in:
        copy.wait_recv()
    g_c[...] = (g_mine[...] + g_core[...].astype(F32)).astype(BF16)
    gy_in = []
    for k in (1, 2, 3):
        there = (y + k) % 4
        gy_in.append(
            remote(g_c.at[:, pl.ds(48 * there, 48)], g_y.at[y], S_GY + k - 1, at_y(k))
        )
    g_y[y] = g_c[:, pl.ds(48 * y, 48), :]

    for copy in tz_in:
        copy.wait_recv()
    total = t_z[0]
    for k in range(1, 8):
        total = total + t_z[k]
    t_x[x] = total
    tx_in = [remote(t_x.at[x], t_x.at[x], S_TX + k - 1, at_x(k)) for k in (1, 2, 3)]

    for copy in gy_in:
        copy.wait_recv()
    piece = g_y[0].astype(F32)
    for k in (1, 2, 3):
        piece = piece + g_y[k].astype(F32)
    g_zs[...] = piece.astype(BF16)
    gz_in = []
    for k in (4, 3, 5, 2, 6, 1, 7):
        there = (zi + k) % 8
        gz_in.append(remote(g_zs.at[there // 4], g_z.at[zi], S_GZ + k - 1, at_z(k)))
    g_z[zi] = g_zs[zh]

    for copy in tx_in:
        copy.wait_recv()
    table_out[...] = (t_x[0] + t_x[1]) + (t_x[2] + t_x[3])

    for copy in gz_in:
        copy.wait_recv()
    piece = g_z[0].astype(F32)
    for k in range(1, 8):
        piece = piece + g_z[k].astype(F32)
    g_oy[y] = piece.astype(BF16)
    oy_in = [remote(g_oy.at[y], g_oy.at[y], S_OY + k - 1, at_y(k)) for k in (1, 2, 3)]
    for copy in oy_in:
        copy.wait_recv()
    oc_in = remote(g_oy, g_oc, S_OC, sibling)
    oc_in.wait_recv()
    grad_out[core] = g_oy[...]
    grad_out[1 - core] = g_oc[...]
    for copy in sends:
        copy.wait_send()


def finish(att_ref, pieces_ref, table_ref, att_out, grad_out, table_out):
    att_out[0] = att_ref[...]
    for k in range(2):
        for n in range(4):
            grad_out[48 * n : 48 * n + 48, 384 * k : 384 * k + 384] = pieces_ref[k, n].astype(F32)
    for h in range(2):
        table_out[:, h, :] = table_ref[:, 32 * h : 32 * h + 32]


def local(features, w_qkv, buckets, cell_ids, bias_table, d_attended):
    types, levels, _ = bias_table.shape
    vmem = pl.BlockSpec(memory_space=pltpu.VMEM)
    hbm = pl.BlockSpec(memory_space=pl.ANY)
    smem = pl.BlockSpec(memory_space=pltpu.SMEM)
    scratch = [
        pltpu.VMEM((192, 256), BF16),
        pltpu.VMEM((256, 192), BF16),
        pltpu.VMEM((256, 256), BF16),
        pltpu.VMEM((32, 2, 32), F32),
        pltpu.VMEM((8, 128), F32),
        pltpu.VMEM((2, TPAD, 128), F32),
        pltpu.VMEM((4, TPAD, 128), F32),
        pltpu.VMEM((1536, 768), BF16),
        pltpu.VMEM((8, 64, 192), BF16),
        pltpu.VMEM((192, 256), BF16),
        pltpu.VMEM((4, 128, 128), BF16),
        pltpu.VMEM((4, 128, 128), BF16),
        pltpu.VMEM((4, TPAD, 128), F32),
        pltpu.VMEM((2, 64, 256), BF16),
        pltpu.VMEM((2, 64, 128), BF16),
        pltpu.VMEM((128, 128), BF16),
        pltpu.VMEM((18, 128, 256), BF16),
        pltpu.VMEM((NWIN, 128, 128), BF16),
        pltpu.VMEM((NWIN, 128, 128), F32),
        pltpu.VMEM((TPAD, 128), F32),
        pltpu.VMEM((TPAD, 128), F32),
        pltpu.VMEM((4, TPAD, 128), F32),
        pltpu.VMEM((4, TPAD, 128), F32),
        pltpu.VMEM((4, 128, 128), F32),
        pltpu.VMEM((4, 128, 128), BF16),
        pltpu.VMEM((4, 128, 128), BF16),
        pltpu.VMEM((4, TPAD, 128), F32),
        pltpu.VMEM((4, TPAD, 128), F32),
        pltpu.VMEM((18, 128, 256), BF16),
        pltpu.VMEM((18, 128, 256), BF16),
        pltpu.VMEM((4, 2, 128, 256), BF16),
        pltpu.VMEM((4, 128, 128), BF16),
        pltpu.VMEM((2, 256, 384), BF16),
        pltpu.VMEM((2, 192, 384), BF16),
        pltpu.VMEM((2, 192, 384), F32),
        pltpu.VMEM((2, 192, 384), BF16),
        pltpu.VMEM((2, 192, 384), BF16),
        pltpu.VMEM((4, 2, 48, 384), BF16),
        pltpu.VMEM((2, 48, 384), BF16),
        pltpu.VMEM((8, 48, 384), BF16),
        pltpu.VMEM((4, 48, 384), BF16),
        pltpu.VMEM((4, 48, 384), BF16),
        pltpu.VMEM((2, 32, 128), F32),
        pltpu.VMEM((4, 32, 128), F32),
        pltpu.VMEM((8, 32, 128), F32),
        pltpu.VMEM((4, 32, 128), F32),
        pltpu.SemaphoreType.DMA((4,)),
        pltpu.SemaphoreType.DMA((N_SEM,)),
        pltpu.SemaphoreType.DMA((N_SEM,)),
    ]
    att, grad, table = pl.pallas_call(
        kernel,
        out_shape=(
            jax.ShapeDtypeStruct((256, 256), BF16),
            jax.ShapeDtypeStruct((2, 4, 48, 384), BF16),
            jax.ShapeDtypeStruct((types, 128), F32),
        ),
        in_specs=[hbm, hbm, smem, smem, hbm, hbm],
        out_specs=(vmem, vmem, vmem),
        scratch_shapes=scratch,
        compiler_params=pltpu.CompilerParams(collective_id=0, has_side_effects=True),
    )(features.T, w_qkv, buckets, cell_ids, bias_table.transpose(0, 2, 1), d_attended)
    att, grad, table = pl.pallas_call(
        finish,
        out_shape=(
            jax.ShapeDtypeStruct((1, 256, 256), BF16),
            jax.ShapeDtypeStruct((192, 768), F32),
            jax.ShapeDtypeStruct((types, HEADS, levels), F32),
        ),
        in_specs=[vmem] * 3,
        out_specs=(vmem,) * 3,
    )(att, grad, table)
    return (att, grad, table.transpose(0, 2, 1))


def solution(mesh):
    in_specs = (
        P("seq", "cell"),
        P(),
        P("cell", "seq", None),
        P("cell"),
        P(),
        P("cell", "seq", None),
    )
    out_specs = (P("cell", "seq", None), P("cell", None), P())
    return jax.shard_map(local, mesh=mesh, in_specs=in_specs, out_specs=out_specs, check_vma=False)
```

```python
import math

import jax
import jax.numpy as jnp
from jax import lax
from jax.experimental import pallas as pl
from jax.experimental.pallas import tpu as pltpu
from jax.sharding import PartitionSpec as P

HEADS = 2
HD = 128
TILE = 128
BT = 16
NSEQ = 32
NWIN = 17
TPAD = 24
NEG = -1e30
FACTOR = 1.0 / math.sqrt(HD)
F32 = jnp.float32
BF16 = jnp.bfloat16

S_FEAT = 0
S_FCROSS = 7
S_DO = 8
S_BIAS = 11
S_KV = 14
S_Q = 17
S_NEAR = 18
S_FAR = 22
S_ATT = 26
S_TT = 29
S_DKV = 32
S_XKV = 40
S_XQ = 43
S_GC = 46
S_TC = 47
S_GY = 48
S_TY = 51
S_GZ = 54
S_TZ = 61
S_TX = 68
S_OY = 71
S_OC = 74
S_SIB = 75
S_GC2 = 83
N_SEM = 84

WIN_OFFSETS = (-4, 4, -3, 3, -2, 2, -1, 1)


def dot_nn(a, b):
    return lax.dot_general(a, b, (((1,), (0,)), ((), ())), preferred_element_type=F32)


def dot_nt(a, b):
    return lax.dot_general(a, b, (((1,), (1,)), ((), ())), preferred_element_type=F32)


def dot_tn(a, b):
    return lax.dot_general(a, b, (((0,), (0,)), ((), ())), preferred_element_type=F32)


class Copy:
    def __init__(self, copy, sends, receives):
        self.copy = copy
        self.sends = sends
        self.receives = receives
        if sends is None:
            copy.start()
        else:
            pl.when(sends)(copy.start)

    def wait_recv(self):
        if self.receives is None:
            self.copy.wait_recv()
        else:
            pl.when(self.receives)(self.copy.wait_recv)

    def wait_send(self):
        if self.sends is None:
            self.copy.wait_send()
        else:
            pl.when(self.sends)(self.copy.wait_send)


def kernel(
    ft_hbm, w_hbm, buckets_ref, ids_ref, tbl_hbm, dout_hbm,
    att_out, grad_out, table_out,
    ft_ref, feat_ref, dout_ref, tbl_ref, row_buf, oh_buf, bias_ref, w_ref, fbuf, fcross, dot_src, dot_buf, bias_buf, proj_kv, proj_q, q_buf, kvw,
    e0_buf, o_buf, m_buf, l_buf, d_buf, w_buf, dof_buf,
    att_src, att_buf, tt_src, tt_buf, dkvw, dkv_in, dkv_x, dq_x, d3,
    g_src, g_mine, g_core, g_c, g_y, g_zs, g_z, g_oy, g_oc,
    t_c, t_y, t_z, t_x, in_sem, send_sem, recv_sem,
):
    cell = lax.axis_index("cell")
    seq = lax.axis_index("seq")
    zh = cell // 4
    x = cell % 4
    z_lo = seq // 8
    y = (seq // 2) % 4
    core = seq % 2
    zi = zh * 4 + z_lo
    head = x % 2
    half = x // 2

    def at_x(k):
        return (zh * 4 + (x + k) % 4, seq)

    def at_cross(k):
        return ((1 - zh) * 4 + (x + k) % 4, seq)

    def at_seq(o):
        return (cell, (seq + o + NSEQ) % NSEQ)

    def at_y(k):
        return (cell, z_lo * 8 + ((y + k) % 4) * 2 + core)

    def at_z(k):
        there = (zi + k) % 8
        return ((there // 4) * 4 + x, (there % 4) * 8 + y * 2 + core)

    sibling = (cell, seq + 1 - 2 * core)

    ft_copy = pltpu.make_async_copy(ft_hbm, ft_ref, in_sem.at[0])
    ft_copy.start()
    barrier = pltpu.get_barrier_semaphore()
    greet = [at_cross(k) for k in range(4)] + [at_x(k) for k in (1, 2, 3)]
    greet += [sibling]
    greet += [at_y(k) for k in (1, 2, 3)] + [at_z(k) for k in range(1, 8)]
    for peer in greet:
        pl.semaphore_signal(barrier, inc=1, device_id=peer, device_id_type=pl.DeviceIdType.MESH)
    chip = seq // 2

    def chip_in(d):
        return (chip + d >= 0) & (chip + d < NSEQ // 2)

    def seq_in(o):
        return (seq + o >= 0) & (seq + o < NSEQ)

    expected = len(greet)
    for o in WIN_OFFSETS:
        @pl.when(seq_in(o))
        def _():
            pl.semaphore_signal(
                barrier, inc=1, device_id=at_seq(o), device_id_type=pl.DeviceIdType.MESH
            )

        expected = expected + seq_in(o).astype(jnp.int32)

    sends = []

    def remote(src, dst, slot, peer, if_send=None, if_recv=None):
        copy = pltpu.make_async_remote_copy(
            src_ref=src,
            dst_ref=dst,
            send_sem=send_sem.at[slot],
            recv_sem=recv_sem.at[slot],
            device_id=peer,
            device_id_type=pl.DeviceIdType.MESH,
        )
        copy = Copy(copy, if_send, if_recv)
        sends.append(copy)
        return copy

    dout_copy = pltpu.make_async_copy(dout_hbm.at[0], dout_ref, in_sem.at[1])
    dout_copy.start()
    tbl_copy = pltpu.make_async_copy(tbl_hbm, tbl_ref, in_sem.at[2])
    tbl_copy.start()
    w_copy = pltpu.make_async_copy(w_hbm, w_ref, in_sem.at[3])
    w_copy.start()
    ft_copy.wait()
    feat = ft_ref[...].astype(F32).T.astype(BF16)
    for n in range(4):
        rows = feat[64 * n : 64 * n + 64]
        feat_ref[n, 0:64, :] = rows[:, 0:128]
        feat_ref[n, 64:96, 0:64] = rows[0:32, 128:192]
        feat_ref[n, 64:96, 64:128] = rows[32:64, 128:192]
    pl.semaphore_wait(barrier, expected)

    feat_in = {}
    for k in (2, 1, 3, 0):
        there = (x + k) % 4
        feat_in[1, k] = remote(feat_ref.at[there], fbuf.at[cell], S_FEAT + k, at_cross(k))
    for k in (1, 3, 2):
        there = (x + k) % 4
        feat_in[0, k] = remote(feat_ref.at[there], fbuf.at[cell], S_FEAT + 3 + k, at_x(k))
    dout_copy.wait()
    for piece in range(4):
        r, h = piece // 2, piece % 2
        block = dout_ref[128 * r : 128 * r + 128, 128 * h : 128 * h + 128]
        dot_src[piece] = block.astype(F32).T.astype(BF16)
    lane = lax.broadcasted_iota(jnp.int32, (1, 128), 1)
    oh_buf[...] = jnp.zeros((2, TPAD, 128), F32)
    row_buf[...] = jnp.zeros((8, 128), F32)
    for r in range(2):
        for o in range(BT):
            oh_buf[r, r + o : r + o + 1, :] = (lane == buckets_ref[0, r, o]).astype(F32)
    tbl_copy.wait()
    hit = (lax.broadcasted_iota(jnp.int32, (32, 128), 0) == ids_ref[0]).astype(F32)
    tile_at = lax.broadcasted_iota(jnp.int32, (TPAD, 128), 0)
    global_tile = 2 * seq - 8 + tile_at
    in_range = (global_tile >= 0) & (global_tile < 2 * NSEQ)
    for h in range(2):
        row_buf[h : h + 1, 0:32] = jnp.sum(
            jnp.where(hit[:, 0:32] > 0.0, tbl_ref[:, h, :], 0.0), axis=0, keepdims=True
        )
        for r in range(2):
            level = jnp.sum(oh_buf[r] * row_buf[h : h + 1, :], axis=1, keepdims=True)
            valid = in_range & (tile_at >= r) & (tile_at < r + BT)
            bias_ref[2 * r + h] = jnp.where(valid, jnp.broadcast_to(level, (TPAD, 128)), NEG)

    do_in = []
    bias_in = []
    for k in (1, 2, 3):
        there = (x + k) % 4
        do_in.append(remote(dot_src.at[there], dot_buf.at[x], S_DO + k - 1, at_x(k)))
        bias_in.append(remote(bias_ref.at[there], bias_buf.at[x], S_BIAS + k - 1, at_x(k)))
    cross_in = remote(ft_ref, fcross, S_FCROSS, at_cross(0))

    dot_buf[x] = dot_src[x]
    bias_buf[x] = bias_ref[x]
    fbuf[cell] = feat_ref[x]
    for t in range(18):
        tile = 2 * seq - 8 + t

        @pl.when((tile < 0) | (tile >= 2 * NSEQ))
        def _():
            kvw[t] = jnp.zeros((128, 256), BF16)
            dkv_in[t] = jnp.zeros((128, 256), BF16)

    w_copy.wait()

    def project(c):
        rows = fbuf[c]
        low = pl.multiple_of(192 * c, 64)
        tail = jnp.concatenate([rows[64:96, 0:64], rows[64:96, 64:128]], axis=0)
        return dot_nn(rows[0:64], w_ref[pl.ds(low, 128), :]) + dot_nn(
            tail, w_ref[pl.ds(pl.multiple_of(low + 128, 64), 64), :]
        )

    proj = project(cell)
    for z, k in ((0, 1), (0, 3), (0, 2), (1, 2), (1, 1), (1, 3), (1, 0)):
        feat_in[z, k].wait_recv()
        half_from = zh if z == 0 else 1 - zh
        proj = proj + project(half_from * 4 + (x - k + 4) % 4)
    projected = proj.astype(BF16)
    for h in range(2):
        proj_q[h] = projected[:, 128 * h : 128 * h + 128]
        proj_kv[h, :, 0:128] = projected[:, 256 + 128 * h : 384 + 128 * h]
        proj_kv[h, :, 128:256] = projected[:, 512 + 128 * h : 640 + 128 * h]

    my_tile = 8 + x // 2
    my_rows = pl.ds(64 * (x % 2), 64)
    kv_in = []
    for k in (1, 2, 3):
        there = (x + k) % 4
        kv_in.append(
            remote(proj_kv.at[there % 2], kvw.at[my_tile, my_rows], S_KV + k - 1, at_x(k))
        )
    mate = (zh * 4 + x + 1 - 2 * (x % 2), seq)
    q_in = remote(proj_q.at[1 - head], q_buf.at[my_rows], S_Q, mate)
    kvw[my_tile, my_rows] = proj_kv[head]
    q_buf[my_rows] = proj_q[head]
    for copy in kv_in:
        copy.wait_recv()

    def relay(src_tile, dst_tile, slot, if_send=None, if_recv=None):
        return remote(
            kvw.at[src_tile], kvw.at[dst_tile], slot, sibling, if_send, if_recv
        )

    near = {}
    far = {}
    mate_in = {}
    pairs = [(t, d) for t in range(2) for d in (-1, 1)]
    for n, (t, d) in enumerate(pairs):
        near[-d, t] = remote(
            kvw.at[8 + t],
            kvw.at[8 - 4 * d + t],
            S_NEAR + n,
            at_seq(2 * d),
            chip_in(d),
            chip_in(-d),
        )
    for t in range(2):
        mate_in[0, t] = relay(8 + t, 6 + 4 * core + t, S_SIB + t)

    def pass_on(t):
        for d in (-1, 1):
            near[d, t].wait_recv()
            here = 8 + 4 * d + t
            n = pairs.index((t, d))
            far[2 * d, t] = remote(
                kvw.at[here],
                kvw.at[8 + 8 * d + t],
                S_FAR + n,
                at_seq(-2 * d),
                chip_in(d) & chip_in(-d),
                chip_in(2 * d),
            )
            mate_in[d, t] = relay(
                here, 6 + 4 * d + 4 * core + t, S_SIB + 2 + n, chip_in(d), chip_in(d)
            )

    def pass_far(t):
        for d in (-2, 2):
            far[d, t].wait_recv()
        mate_in[2, t] = relay(
            16 - 16 * core + t,
            14 - 12 * core + t,
            S_SIB + 6 + t,
            chip_in(2 - 4 * core),
            chip_in(4 * core - 2),
        )

    q_in.wait_recv()
    for copy in do_in + bias_in:
        copy.wait_recv()

    q_tile = q_buf[...]
    for c in range(4):
        dof_buf[c] = dot_buf[c].astype(F32)
    m_buf[...] = jnp.zeros((TPAD, 128), F32)
    l_buf[...] = jnp.zeros((TPAD, 128), F32)
    d_buf[...] = jnp.zeros((4, TPAD, 128), F32)

    def forward_tile(t):
        keys = kvw[t, :, 0:128]
        values = kvw[t, :, 128:256]
        s = dot_nt(keys, q_tile) * FACTOR
        top = jnp.max(s, axis=0, keepdims=True)
        e0 = jnp.exp(s - top)
        m_buf[pl.ds(t, 1), :] = top
        l_buf[pl.ds(t, 1), :] = jnp.sum(e0, axis=0, keepdims=True)
        e0b = e0.astype(BF16)
        e0_buf[t] = e0b
        o_t = dot_tn(values, e0b)
        o_buf[t] = o_t
        for c in range(4):
            d_buf[c, pl.ds(t, 1), :] = jnp.sum(dof_buf[c] * o_t, axis=0, keepdims=True)

    forward_tile(8)
    pass_on(0)
    forward_tile(9)
    pass_on(1)
    for t in range(2):
        mate_in[0, t].wait_recv()
        forward_tile(10 - 4 * core + t)
    for t in range(2):
        for d in (-1, 1):
            forward_tile(8 + 4 * d + t)
    pass_far(0)
    for t in range(2):
        for d in (-1, 1):
            mate_in[d, t].wait_recv()
            forward_tile(10 + 4 * d - 4 * core + t)
    pass_far(1)
    forward_tile(0)
    forward_tile(1)
    forward_tile(16)
    for t in range(2):
        mate_in[2, t].wait_recv()
        forward_tile(2 + 12 * core + t)

    m_all = m_buf[...]
    l_all = l_buf[...]
    big = jnp.zeros((TPAD, 128), F32)
    att_in = []
    tt_in = []
    for c in range(4):
        z = m_all + bias_buf[c]
        top = jnp.max(z, axis=0, keepdims=True)
        ex = jnp.exp(z - top)
        mass = jnp.sum(ex * l_all, axis=0, keepdims=True)
        w_c = ex / mass
        w_buf[c] = w_c
        acc = jnp.zeros((128, 128), F32)
        for t in range(NWIN):
            acc = acc + w_c[t : t + 1, :] * o_buf[t]
        accb = acc.astype(BF16)
        att_src[c] = acc.T.astype(BF16)
        delta = jnp.sum(dof_buf[c] * accb.astype(F32), axis=0, keepdims=True)
        big = big + w_c * delta
        tt_src[c] = w_c * (d_buf[c] - delta * l_all)
    for k in (1, 2, 3):
        there = (x + k) % 4
        att_in.append(remote(att_src.at[there], att_buf.at[x], S_ATT + k - 1, at_x(k)))
        tt_in.append(remote(tt_src.at[there], tt_buf.at[x], S_TT + k - 1, at_x(k)))
    att_buf[x] = att_src[x]
    tt_buf[x] = tt_src[x]

    dq_acc = jnp.zeros((128, 128), F32)
    dkv_get = {}
    for slot in (0, 8, 1, 7, 2, 6, 3, 5, 4):
        for t in (2 * slot, 2 * slot + 1):
            if t >= NWIN:
                continue
            g_t = w_buf[0, t : t + 1, :] * dof_buf[0]
            for c in (1, 2, 3):
                g_t = g_t + w_buf[c, t : t + 1, :] * dof_buf[c]
            gb = g_t.astype(BF16)
            e0b = e0_buf[t]
            dp = dot_nn(kvw[t, :, 128:256], gb)
            ds = (e0b.astype(F32) * (dp - big[t : t + 1, :])).astype(BF16)
            dkvw[t, :, 0:128] = (dot_nn(ds, q_tile) * FACTOR).astype(BF16)
            dkvw[t, :, 128:256] = dot_nt(e0b, gb).astype(BF16)
            dq_acc = dq_acc + dot_tn(ds, kvw[t, :, 0:128])
        o = slot - 4
        if o != 0:
            n = WIN_OFFSETS.index(o)
            count = 1 if o == 4 else 2
            dkv_get[4 - o] = remote(
                dkvw.at[pl.ds(2 * slot, count)],
                dkv_in.at[pl.ds(2 * (4 - o), count)],
                S_DKV + n,
                at_seq(o),
                seq_in(o),
                seq_in(-o),
            )
    dq_x[x] = (dq_acc * FACTOR).astype(BF16)
    xq_in = [remote(dq_x.at[x], dq_x.at[x], S_XQ + k - 1, at_x(k)) for k in (1, 2, 3)]

    for copy in tt_in:
        copy.wait_recv()
    ones = jnp.ones((8, 128), F32)
    rows = []
    for h in range(2):
        row = jnp.zeros((8, 128), F32)
        for r in range(2):
            sums = lax.dot_general(
                ones, tt_buf[2 * r + h], (((1,), (1,)), ((), ())),
                precision=lax.Precision.HIGHEST, preferred_element_type=F32,
            )
            row = row + lax.dot_general(
                sums, oh_buf[r], (((1,), (0,)), ((), ())),
                precision=lax.Precision.HIGHEST, preferred_element_type=F32,
            )
        rows.append(row)
    both_heads = rows[0] + pltpu.roll(rows[1], 32, axis=1)
    t_c[core] = hit * both_heads[0:1, :]
    tc_in = remote(t_c.at[core], t_c.at[core], S_TC, sibling)

    for copy in att_in:
        copy.wait_recv()
    for piece in range(4):
        r, h = piece // 2, piece % 2
        att_out[128 * r : 128 * r + 128, 128 * h : 128 * h + 128] = att_buf[piece]

    for slot in (4, 3, 5, 2, 6, 1, 7, 0, 8):
        if slot != 4:
            dkv_get[slot].wait_recv()
    for t in range(2):
        acc = dkvw[8 + t].astype(F32)
        for slot in (3, 5, 2, 6, 1, 7, 0, 8):
            if slot == 0 and t == 1:
                continue
            acc = acc + dkv_in[2 * slot + t].astype(F32)
        dkv_x[x, t] = acc.astype(BF16)
    xkv_in = [remote(dkv_x.at[x], dkv_x.at[x], S_XKV + k - 1, at_x(k)) for k in (1, 2, 3)]

    tc_in.wait_recv()
    t_y[y] = t_c[0] + t_c[1]
    ty_in = [remote(t_y.at[y], t_y.at[y], S_TY + k - 1, at_y(k)) for k in (1, 2, 3)]

    for copy in xq_in + xkv_in:
        copy.wait_recv()
    for t in range(2):
        at_rows = slice(128 * t, 128 * t + 128)
        for h in range(2):
            d3[0, at_rows, 128 * h : 128 * h + 128] = dq_x[2 * t + h]
            both = dkv_x[h, t].astype(F32) + dkv_x[2 + h, t].astype(F32)
            bothb = both.astype(BF16)
            d3[h, at_rows, 256 - 256 * h : 384 - 256 * h] = bothb[:, 0:128]
            d3[1, at_rows, 128 + 128 * h : 256 + 128 * h] = bothb[:, 128:256]

    cross_in.wait_recv()
    theirs = d3[1 - core]
    g_src[zh] = dot_nn(ft_ref[...], theirs).astype(BF16)
    gc_in = [remote(g_src.at[zh], g_core.at[zh], S_GC, sibling)]
    g_src[1 - zh] = dot_nn(fcross[...], theirs).astype(BF16)
    gc_in.append(remote(g_src.at[1 - zh], g_core.at[1 - zh], S_GC2, sibling))
    mine = d3[core]
    g_mine[zh] = dot_nn(ft_ref[...], mine)
    g_mine[1 - zh] = dot_nn(fcross[...], mine)

    for copy in ty_in:
        copy.wait_recv()
    t_z[zi] = (t_y[0] + t_y[1]) + (t_y[2] + t_y[3])
    tz_in = [remote(t_z.at[zi], t_z.at[zi], S_TZ + k - 1, at_z(k)) for k in range(1, 8)]

    for copy in gc_in:
        copy.wait_recv()
    g_c[...] = (g_mine[...] + g_core[...].astype(F32)).astype(BF16)
    gy_in = []
    for k in (1, 2, 3):
        there = (y + k) % 4
        gy_in.append(
            remote(g_c.at[:, pl.ds(48 * there, 48)], g_y.at[y], S_GY + k - 1, at_y(k))
        )
    g_y[y] = g_c[:, pl.ds(48 * y, 48), :]

    for copy in tz_in:
        copy.wait_recv()
    total = t_z[0]
    for k in range(1, 8):
        total = total + t_z[k]
    t_x[x] = total
    tx_in = [remote(t_x.at[x], t_x.at[x], S_TX + k - 1, at_x(k)) for k in (1, 2, 3)]

    for copy in gy_in:
        copy.wait_recv()
    piece = g_y[0].astype(F32)
    for k in (1, 2, 3):
        piece = piece + g_y[k].astype(F32)
    g_zs[...] = piece.astype(BF16)
    gz_in = []
    for k in (4, 3, 5, 2, 6, 1, 7):
        there = (zi + k) % 8
        gz_in.append(remote(g_zs.at[there // 4], g_z.at[zi], S_GZ + k - 1, at_z(k)))
    g_z[zi] = g_zs[zh]

    for copy in tx_in:
        copy.wait_recv()
    table_out[...] = (t_x[0] + t_x[1]) + (t_x[2] + t_x[3])

    for copy in gz_in:
        copy.wait_recv()
    piece = g_z[0].astype(F32)
    for k in range(1, 8):
        piece = piece + g_z[k].astype(F32)
    g_oy[y] = piece.astype(BF16)
    oy_in = [remote(g_oy.at[y], g_oy.at[y], S_OY + k - 1, at_y(k)) for k in (1, 2, 3)]
    for copy in oy_in:
        copy.wait_recv()
    oc_in = remote(g_oy, g_oc, S_OC, sibling)
    oc_in.wait_recv()
    grad_out[core] = g_oy[...]
    grad_out[1 - core] = g_oc[...]
    for copy in sends:
        copy.wait_send()


def finish(att_ref, pieces_ref, table_ref, att_out, grad_out, table_out):
    att_out[0] = att_ref[...]
    for k in range(2):
        for n in range(4):
            grad_out[48 * n : 48 * n + 48, 384 * k : 384 * k + 384] = pieces_ref[k, n].astype(F32)
    for h in range(2):
        table_out[:, h, :] = table_ref[:, 32 * h : 32 * h + 32]


def local(features, w_qkv, buckets, cell_ids, bias_table, d_attended):
    types, levels, _ = bias_table.shape
    vmem = pl.BlockSpec(memory_space=pltpu.VMEM)
    hbm = pl.BlockSpec(memory_space=pl.ANY)
    smem = pl.BlockSpec(memory_space=pltpu.SMEM)
    scratch = [
        pltpu.VMEM((192, 256), BF16),
        pltpu.VMEM((4, 96, 128), BF16),
        pltpu.VMEM((256, 256), BF16),
        pltpu.VMEM((32, 2, 32), F32),
        pltpu.VMEM((8, 128), F32),
        pltpu.VMEM((2, TPAD, 128), F32),
        pltpu.VMEM((4, TPAD, 128), F32),
        pltpu.VMEM((1536, 768), BF16),
        pltpu.VMEM((8, 96, 128), BF16),
        pltpu.VMEM((192, 256), BF16),
        pltpu.VMEM((4, 128, 128), BF16),
        pltpu.VMEM((4, 128, 128), BF16),
        pltpu.VMEM((4, TPAD, 128), F32),
        pltpu.VMEM((2, 64, 256), BF16),
        pltpu.VMEM((2, 64, 128), BF16),
        pltpu.VMEM((128, 128), BF16),
        pltpu.VMEM((18, 128, 256), BF16),
        pltpu.VMEM((NWIN, 128, 128), BF16),
        pltpu.VMEM((NWIN, 128, 128), F32),
        pltpu.VMEM((TPAD, 128), F32),
        pltpu.VMEM((TPAD, 128), F32),
        pltpu.VMEM((4, TPAD, 128), F32),
        pltpu.VMEM((4, TPAD, 128), F32),
        pltpu.VMEM((4, 128, 128), F32),
        pltpu.VMEM((4, 128, 128), BF16),
        pltpu.VMEM((4, 128, 128), BF16),
        pltpu.VMEM((4, TPAD, 128), F32),
        pltpu.VMEM((4, TPAD, 128), F32),
        pltpu.VMEM((18, 128, 256), BF16),
        pltpu.VMEM((18, 128, 256), BF16),
        pltpu.VMEM((4, 2, 128, 256), BF16),
        pltpu.VMEM((4, 128, 128), BF16),
        pltpu.VMEM((2, 256, 384), BF16),
        pltpu.VMEM((2, 192, 384), BF16),
        pltpu.VMEM((2, 192, 384), F32),
        pltpu.VMEM((2, 192, 384), BF16),
        pltpu.VMEM((2, 192, 384), BF16),
        pltpu.VMEM((4, 2, 48, 384), BF16),
        pltpu.VMEM((2, 48, 384), BF16),
        pltpu.VMEM((8, 48, 384), BF16),
        pltpu.VMEM((4, 48, 384), BF16),
        pltpu.VMEM((4, 48, 384), BF16),
        pltpu.VMEM((2, 32, 128), F32),
        pltpu.VMEM((4, 32, 128), F32),
        pltpu.VMEM((8, 32, 128), F32),
        pltpu.VMEM((4, 32, 128), F32),
        pltpu.SemaphoreType.DMA((4,)),
        pltpu.SemaphoreType.DMA((N_SEM,)),
        pltpu.SemaphoreType.DMA((N_SEM,)),
    ]
    att, grad, table = pl.pallas_call(
        kernel,
        out_shape=(
            jax.ShapeDtypeStruct((256, 256), BF16),
            jax.ShapeDtypeStruct((2, 4, 48, 384), BF16),
            jax.ShapeDtypeStruct((types, 128), F32),
        ),
        in_specs=[hbm, hbm, smem, smem, hbm, hbm],
        out_specs=(vmem, vmem, vmem),
        scratch_shapes=scratch,
        compiler_params=pltpu.CompilerParams(collective_id=0, has_side_effects=True),
    )(features.T, w_qkv, buckets, cell_ids, bias_table.transpose(0, 2, 1), d_attended)
    att, grad, table = pl.pallas_call(
        finish,
        out_shape=(
            jax.ShapeDtypeStruct((1, 256, 256), BF16),
            jax.ShapeDtypeStruct((192, 768), F32),
            jax.ShapeDtypeStruct((types, HEADS, levels), F32),
        ),
        in_specs=[vmem] * 3,
        out_specs=(vmem,) * 3,
    )(att, grad, table)
    return (att, grad, table.transpose(0, 2, 1))


def solution(mesh):
    in_specs = (
        P("seq", "cell"),
        P(),
        P("cell", "seq", None),
        P("cell"),
        P(),
        P("cell", "seq", None),
    )
    out_specs = (P("cell", "seq", None), P("cell", None), P())
    return jax.shard_map(local, mesh=mesh, in_specs=in_specs, out_specs=out_specs, check_vma=False)
```

```python
import math

import jax
import jax.numpy as jnp
from jax import lax
from jax.experimental import pallas as pl
from jax.experimental.pallas import tpu as pltpu
from jax.sharding import PartitionSpec as P

HEADS = 2
HD = 128
TILE = 128
BT = 16
NSEQ = 32
NWIN = 17
TPAD = 24
NEG = -1e30
FACTOR = 1.0 / math.sqrt(HD)
F32 = jnp.float32
BF16 = jnp.bfloat16

S_FEAT = 0
S_FCROSS = 7
S_DO = 8
S_BIAS = 11
S_KV = 14
S_Q = 17
S_NEAR = 18
S_FAR = 22
S_ATT = 26
S_TT = 29
S_DKV = 32
S_XKV = 40
S_XQ = 43
S_GC = 46
S_TC = 47
S_GY = 48
S_TY = 51
S_GZ = 54
S_TZ = 61
S_TX = 68
S_OY = 71
S_OC = 74
S_SIB = 75
S_GC2 = 83
S_XKV2 = 84
S_DNEAR = 87
S_DFAR = 91
N_SEM = 95

CHIP_STEPS = (-2, 2)


def dot_nn(a, b):
    return lax.dot_general(a, b, (((1,), (0,)), ((), ())), preferred_element_type=F32)


def dot_nt(a, b):
    return lax.dot_general(a, b, (((1,), (1,)), ((), ())), preferred_element_type=F32)


def dot_tn(a, b):
    return lax.dot_general(a, b, (((0,), (0,)), ((), ())), preferred_element_type=F32)


class Copy:
    def __init__(self, copy, sends, receives):
        self.copy = copy
        self.sends = sends
        self.receives = receives
        if sends is None:
            copy.start()
        else:
            pl.when(sends)(copy.start)

    def wait_recv(self):
        if self.receives is None:
            self.copy.wait_recv()
        else:
            pl.when(self.receives)(self.copy.wait_recv)

    def wait_send(self):
        if self.sends is None:
            self.copy.wait_send()
        else:
            pl.when(self.sends)(self.copy.wait_send)


def kernel(
    ft_hbm, w_hbm, buckets_ref, ids_ref, tbl_hbm, dout_hbm,
    att_out, grad_out, table_out,
    ft_ref, feat_ref, dout_ref, tbl_ref, row_buf, oh_buf, bias_ref, w_ref, fbuf, fcross, dot_src, dot_buf, bias_buf, proj_kv, proj_q, q_buf, kvw,
    e0_buf, o_buf, m_buf, l_buf, d_buf, w_buf, dof_buf,
    att_src, att_buf, tt_src, tt_buf, dkvw, mate_dkv, far_src, far_in, near_src, near_in, dkv_x, dq_x, d3,
    g_src, g_mine, g_core, g_c, g_y, g_zs, g_z, g_oy, g_oc,
    t_c, t_y, t_z, t_x, in_sem, send_sem, recv_sem,
):
    cell = lax.axis_index("cell")
    seq = lax.axis_index("seq")
    zh = cell // 4
    x = cell % 4
    z_lo = seq // 8
    y = (seq // 2) % 4
    core = seq % 2
    zi = zh * 4 + z_lo
    head = x % 2
    half = x // 2

    def at_x(k):
        return (zh * 4 + (x + k) % 4, seq)

    def at_cross(k):
        return ((1 - zh) * 4 + (x + k) % 4, seq)

    def at_seq(o):
        return (cell, (seq + o + NSEQ) % NSEQ)

    def at_y(k):
        return (cell, z_lo * 8 + ((y + k) % 4) * 2 + core)

    def at_z(k):
        there = (zi + k) % 8
        return ((there // 4) * 4 + x, (there % 4) * 8 + y * 2 + core)

    sibling = (cell, seq + 1 - 2 * core)

    ft_copy = pltpu.make_async_copy(ft_hbm, ft_ref, in_sem.at[0])
    ft_copy.start()
    barrier = pltpu.get_barrier_semaphore()
    greet = [at_cross(k) for k in range(4)] + [at_x(k) for k in (1, 2, 3)]
    greet += [sibling]
    greet += [at_y(k) for k in (1, 2, 3)] + [at_z(k) for k in range(1, 8)]
    for peer in greet:
        pl.semaphore_signal(barrier, inc=1, device_id=peer, device_id_type=pl.DeviceIdType.MESH)
    chip = seq // 2

    def chip_in(d):
        return (chip + d >= 0) & (chip + d < NSEQ // 2)

    def seq_in(o):
        return (seq + o >= 0) & (seq + o < NSEQ)

    expected = len(greet)
    for o in CHIP_STEPS:
        @pl.when(seq_in(o))
        def _():
            pl.semaphore_signal(
                barrier, inc=1, device_id=at_seq(o), device_id_type=pl.DeviceIdType.MESH
            )

        expected = expected + seq_in(o).astype(jnp.int32)

    sends = []

    def remote(src, dst, slot, peer, if_send=None, if_recv=None):
        copy = pltpu.make_async_remote_copy(
            src_ref=src,
            dst_ref=dst,
            send_sem=send_sem.at[slot],
            recv_sem=recv_sem.at[slot],
            device_id=peer,
            device_id_type=pl.DeviceIdType.MESH,
        )
        copy = Copy(copy, if_send, if_recv)
        sends.append(copy)
        return copy

    dout_copy = pltpu.make_async_copy(dout_hbm.at[0], dout_ref, in_sem.at[1])
    dout_copy.start()
    tbl_copy = pltpu.make_async_copy(tbl_hbm, tbl_ref, in_sem.at[2])
    tbl_copy.start()
    w_copy = pltpu.make_async_copy(w_hbm, w_ref, in_sem.at[3])
    w_copy.start()
    ft_copy.wait()
    feat = ft_ref[...].astype(F32).T.astype(BF16)
    for n in range(4):
        rows = feat[64 * n : 64 * n + 64]
        feat_ref[n, 0:64, :] = rows[:, 0:128]
        feat_ref[n, 64:96, 0:64] = rows[0:32, 128:192]
        feat_ref[n, 64:96, 64:128] = rows[32:64, 128:192]
    pl.semaphore_wait(barrier, expected)

    feat_in = {}
    for k in (2, 1, 3, 0):
        there = (x + k) % 4
        feat_in[1, k] = remote(feat_ref.at[there], fbuf.at[cell], S_FEAT + k, at_cross(k))
    for k in (1, 3, 2):
        there = (x + k) % 4
        feat_in[0, k] = remote(feat_ref.at[there], fbuf.at[cell], S_FEAT + 3 + k, at_x(k))
    dout_copy.wait()
    for piece in range(4):
        r, h = piece // 2, piece % 2
        block = dout_ref[128 * r : 128 * r + 128, 128 * h : 128 * h + 128]
        dot_src[piece] = block.astype(F32).T.astype(BF16)
    lane = lax.broadcasted_iota(jnp.int32, (1, 128), 1)
    oh_buf[...] = jnp.zeros((2, TPAD, 128), F32)
    row_buf[...] = jnp.zeros((8, 128), F32)
    for r in range(2):
        for o in range(BT):
            oh_buf[r, r + o : r + o + 1, :] = (lane == buckets_ref[0, r, o]).astype(F32)
    tbl_copy.wait()
    hit = (lax.broadcasted_iota(jnp.int32, (32, 128), 0) == ids_ref[0]).astype(F32)
    tile_at = lax.broadcasted_iota(jnp.int32, (TPAD, 128), 0)
    global_tile = 2 * seq - 8 + tile_at
    in_range = (global_tile >= 0) & (global_tile < 2 * NSEQ)
    for h in range(2):
        row_buf[h : h + 1, 0:32] = jnp.sum(
            jnp.where(hit[:, 0:32] > 0.0, tbl_ref[:, h, :], 0.0), axis=0, keepdims=True
        )
        for r in range(2):
            level = jnp.sum(oh_buf[r] * row_buf[h : h + 1, :], axis=1, keepdims=True)
            valid = in_range & (tile_at >= r) & (tile_at < r + BT)
            bias_ref[2 * r + h] = jnp.where(valid, jnp.broadcast_to(level, (TPAD, 128)), NEG)

    do_in = []
    bias_in = []
    for k in (1, 2, 3):
        there = (x + k) % 4
        do_in.append(remote(dot_src.at[there], dot_buf.at[x], S_DO + k - 1, at_x(k)))
        bias_in.append(remote(bias_ref.at[there], bias_buf.at[x], S_BIAS + k - 1, at_x(k)))
    cross_in = remote(ft_ref, fcross, S_FCROSS, at_cross(0))

    dot_buf[x] = dot_src[x]
    bias_buf[x] = bias_ref[x]
    fbuf[cell] = feat_ref[x]
    for t in range(18):
        tile = 2 * seq - 8 + t

        @pl.when((tile < 0) | (tile >= 2 * NSEQ))
        def _():
            kvw[t] = jnp.zeros((128, 256), BF16)

    w_copy.wait()

    zero_tile = jnp.zeros((2, 128, 256), BF16)
    dkvw[17] = jnp.zeros((128, 256), BF16)
    mate_dkv[0] = zero_tile
    mate_dkv[5] = zero_tile
    for n, d in enumerate((1, -1)):
        @pl.when(jnp.logical_not(chip_in(d)))
        def _():
            far_in[n] = zero_tile
            near_in[n] = zero_tile

    def project(c):
        rows = fbuf[c]
        low = pl.multiple_of(192 * c, 64)
        tail = jnp.concatenate([rows[64:96, 0:64], rows[64:96, 64:128]], axis=0)
        return dot_nn(rows[0:64], w_ref[pl.ds(low, 128), :]) + dot_nn(
            tail, w_ref[pl.ds(pl.multiple_of(low + 128, 64), 64), :]
        )

    proj = project(cell)
    for z, k in ((0, 1), (0, 3), (0, 2), (1, 2), (1, 1), (1, 3), (1, 0)):
        feat_in[z, k].wait_recv()
        half_from = zh if z == 0 else 1 - zh
        proj = proj + project(half_from * 4 + (x - k + 4) % 4)
    projected = proj.astype(BF16)
    for h in range(2):
        proj_q[h] = projected[:, 128 * h : 128 * h + 128]
        proj_kv[h, :, 0:128] = projected[:, 256 + 128 * h : 384 + 128 * h]
        proj_kv[h, :, 128:256] = projected[:, 512 + 128 * h : 640 + 128 * h]

    my_tile = 8 + x // 2
    my_rows = pl.ds(64 * (x % 2), 64)
    kv_in = []
    for k in (1, 2, 3):
        there = (x + k) % 4
        kv_in.append(
            remote(proj_kv.at[there % 2], kvw.at[my_tile, my_rows], S_KV + k - 1, at_x(k))
        )
    mate = (zh * 4 + x + 1 - 2 * (x % 2), seq)
    q_in = remote(proj_q.at[1 - head], q_buf.at[my_rows], S_Q, mate)
    kvw[my_tile, my_rows] = proj_kv[head]
    q_buf[my_rows] = proj_q[head]
    for copy in kv_in:
        copy.wait_recv()

    def relay(src_tile, dst_tile, slot, if_send=None, if_recv=None):
        return remote(
            kvw.at[src_tile], kvw.at[dst_tile], slot, sibling, if_send, if_recv
        )

    near = {}
    far = {}
    mate_in = {}
    pairs = [(t, d) for t in range(2) for d in (-1, 1)]
    for n, (t, d) in enumerate(pairs):
        near[-d, t] = remote(
            kvw.at[8 + t],
            kvw.at[8 - 4 * d + t],
            S_NEAR + n,
            at_seq(2 * d),
            chip_in(d),
            chip_in(-d),
        )
    for t in range(2):
        mate_in[0, t] = relay(8 + t, 6 + 4 * core + t, S_SIB + t)

    def pass_on(t):
        for d in (-1, 1):
            near[d, t].wait_recv()
            here = 8 + 4 * d + t
            n = pairs.index((t, d))
            far[2 * d, t] = remote(
                kvw.at[here],
                kvw.at[8 + 8 * d + t],
                S_FAR + n,
                at_seq(-2 * d),
                chip_in(d) & chip_in(-d),
                chip_in(2 * d),
            )
            mate_in[d, t] = relay(
                here, 6 + 4 * d + 4 * core + t, S_SIB + 2 + n, chip_in(d), chip_in(d)
            )

    def pass_far(t):
        for d in (-2, 2):
            far[d, t].wait_recv()
        mate_in[2, t] = relay(
            16 - 16 * core + t,
            14 - 12 * core + t,
            S_SIB + 6 + t,
            chip_in(2 - 4 * core),
            chip_in(4 * core - 2),
        )

    q_in.wait_recv()
    for copy in do_in + bias_in:
        copy.wait_recv()

    q_tile = q_buf[...]
    for c in range(4):
        dof_buf[c] = dot_buf[c].astype(F32)
    m_buf[...] = jnp.zeros((TPAD, 128), F32)
    l_buf[...] = jnp.zeros((TPAD, 128), F32)
    d_buf[...] = jnp.zeros((4, TPAD, 128), F32)

    def forward_tile(t):
        keys = kvw[t, :, 0:128]
        values = kvw[t, :, 128:256]
        s = dot_nt(keys, q_tile) * FACTOR
        top = jnp.max(s, axis=0, keepdims=True)
        e0 = jnp.exp(s - top)
        m_buf[pl.ds(t, 1), :] = top
        l_buf[pl.ds(t, 1), :] = jnp.sum(e0, axis=0, keepdims=True)
        e0b = e0.astype(BF16)
        e0_buf[t] = e0b
        o_t = dot_tn(values, e0b)
        o_buf[t] = o_t
        for c in range(4):
            d_buf[c, pl.ds(t, 1), :] = jnp.sum(dof_buf[c] * o_t, axis=0, keepdims=True)

    forward_tile(8)
    pass_on(0)
    forward_tile(9)
    pass_on(1)
    for t in range(2):
        mate_in[0, t].wait_recv()
        forward_tile(10 - 4 * core + t)
    for t in range(2):
        for d in (-1, 1):
            forward_tile(8 + 4 * d + t)
    pass_far(0)
    for t in range(2):
        for d in (-1, 1):
            mate_in[d, t].wait_recv()
            forward_tile(10 + 4 * d - 4 * core + t)
    pass_far(1)
    forward_tile(0)
    forward_tile(1)
    forward_tile(16)
    for t in range(2):
        mate_in[2, t].wait_recv()
        forward_tile(2 + 12 * core + t)

    m_all = m_buf[...]
    l_all = l_buf[...]
    big = jnp.zeros((TPAD, 128), F32)
    att_in = []
    tt_in = []
    for c in range(4):
        z = m_all + bias_buf[c]
        top = jnp.max(z, axis=0, keepdims=True)
        ex = jnp.exp(z - top)
        mass = jnp.sum(ex * l_all, axis=0, keepdims=True)
        w_c = ex / mass
        w_buf[c] = w_c
        acc = jnp.zeros((128, 128), F32)
        for t in range(NWIN):
            acc = acc + w_c[t : t + 1, :] * o_buf[t]
        accb = acc.astype(BF16)
        att_src[c] = acc.T.astype(BF16)
        delta = jnp.sum(dof_buf[c] * accb.astype(F32), axis=0, keepdims=True)
        big = big + w_c * delta
        tt_src[c] = w_c * (d_buf[c] - delta * l_all)
    for k in (1, 2, 3):
        there = (x + k) % 4
        att_in.append(remote(att_src.at[there], att_buf.at[x], S_ATT + k - 1, at_x(k)))
        tt_in.append(remote(tt_src.at[there], tt_buf.at[x], S_TT + k - 1, at_x(k)))
    att_buf[x] = att_src[x]
    tt_buf[x] = tt_src[x]

    dq_acc = jnp.zeros((128, 128), F32)

    def backward_slot(slot, dq_acc):
        for t in (2 * slot, 2 * slot + 1):
            if t >= NWIN:
                continue
            g_t = w_buf[0, t : t + 1, :] * dof_buf[0]
            for c in (1, 2, 3):
                g_t = g_t + w_buf[c, t : t + 1, :] * dof_buf[c]
            gb = g_t.astype(BF16)
            e0b = e0_buf[t]
            dp = dot_nn(kvw[t, :, 128:256], gb)
            ds = (e0b.astype(F32) * (dp - big[t : t + 1, :])).astype(BF16)
            dkvw[t, :, 0:128] = (dot_nn(ds, q_tile) * FACTOR).astype(BF16)
            dkvw[t, :, 128:256] = dot_nt(e0b, gb).astype(BF16)
            dq_acc = dq_acc + dot_tn(ds, kvw[t, :, 0:128])
        return dq_acc

    mate_in = {}
    for slot in (1, 7, 3, 5):
        dq_acc = backward_slot(slot, dq_acc)
        j = slot // 2
        mate_in[j] = remote(
            dkvw.at[pl.ds(2 * slot, 2)], mate_dkv.at[j + 1], S_DKV + j, sibling
        )

    def chip_sum(e, t):
        return dkvw[4 * e + t].astype(F32) + mate_dkv[e + core, t].astype(F32)

    dq_acc = backward_slot(0, dq_acc)
    dq_acc = backward_slot(8, dq_acc)
    mate_in[0].wait_recv()
    mate_in[3].wait_recv()
    far = {}
    for t in range(2):
        for n, (e, d) in enumerate(((0, -1), (4, 1))):
            far_src[n, t] = chip_sum(e, t).astype(BF16)
            far[n, t] = remote(
                far_src.at[n, t],
                far_in.at[n, t],
                S_DFAR + 2 * t + n,
                at_seq(2 * d),
                chip_in(2 * d),
                chip_in(1) & chip_in(-1),
            )
    for slot in (2, 6, 4):
        dq_acc = backward_slot(slot, dq_acc)
    dq_x[x] = (dq_acc * FACTOR).astype(BF16)
    xq_in = [remote(dq_x.at[x], dq_x.at[x], S_XQ + k - 1, at_x(k)) for k in (1, 2, 3)]

    mate_in[1].wait_recv()
    mate_in[2].wait_recv()
    near = {}
    for t in range(2):
        for n, (e, d) in enumerate(((1, -1), (3, 1))):
            far[n, t].wait_recv()
            near_src[n, t] = (chip_sum(e, t) + far_in[n, t].astype(F32)).astype(BF16)
            near[n, t] = remote(
                near_src.at[n, t],
                near_in.at[n, t],
                S_DNEAR + 2 * t + n,
                at_seq(2 * d),
                chip_in(d),
                chip_in(-d),
            )

    for copy in tt_in:
        copy.wait_recv()
    ones = jnp.ones((8, 128), F32)
    rows = []
    for h in range(2):
        row = jnp.zeros((8, 128), F32)
        for r in range(2):
            sums = lax.dot_general(
                ones, tt_buf[2 * r + h], (((1,), (1,)), ((), ())),
                precision=lax.Precision.HIGHEST, preferred_element_type=F32,
            )
            row = row + lax.dot_general(
                sums, oh_buf[r], (((1,), (0,)), ((), ())),
                precision=lax.Precision.HIGHEST, preferred_element_type=F32,
            )
        rows.append(row)
    both_heads = rows[0] + pltpu.roll(rows[1], 32, axis=1)
    t_c[core] = hit * both_heads[0:1, :]
    tc_in = remote(t_c.at[core], t_c.at[core], S_TC, sibling)

    for copy in att_in:
        copy.wait_recv()
    for piece in range(4):
        r, h = piece // 2, piece % 2
        att_out[128 * r : 128 * r + 128, 128 * h : 128 * h + 128] = att_buf[piece]

    xkv_in = []
    for t in range(2):
        for n in range(2):
            near[n, t].wait_recv()
        acc = chip_sum(2, t) + near_in[0, t].astype(F32) + near_in[1, t].astype(F32)
        dkv_x[x, t] = acc.astype(BF16)
        xkv_in.append(
            [
                remote(
                    dkv_x.at[x, t], dkv_x.at[x, t], (S_XKV, S_XKV2)[t] + k - 1, at_x(k)
                )
                for k in (1, 2, 3)
            ]
        )

    tc_in.wait_recv()
    t_y[y] = t_c[0] + t_c[1]
    ty_in = [remote(t_y.at[y], t_y.at[y], S_TY + k - 1, at_y(k)) for k in (1, 2, 3)]

    for copy in xq_in:
        copy.wait_recv()
    for t in range(2):
        for copy in xkv_in[t]:
            copy.wait_recv()
        at_rows = slice(128 * t, 128 * t + 128)
        for h in range(2):
            d3[0, at_rows, 128 * h : 128 * h + 128] = dq_x[2 * t + h]
            both = dkv_x[h, t].astype(F32) + dkv_x[2 + h, t].astype(F32)
            bothb = both.astype(BF16)
            d3[h, at_rows, 256 - 256 * h : 384 - 256 * h] = bothb[:, 0:128]
            d3[1, at_rows, 128 + 128 * h : 256 + 128 * h] = bothb[:, 128:256]

    cross_in.wait_recv()
    theirs = d3[1 - core]
    g_src[zh] = dot_nn(ft_ref[...], theirs).astype(BF16)
    gc_in = [remote(g_src.at[zh], g_core.at[zh], S_GC, sibling)]
    g_src[1 - zh] = dot_nn(fcross[...], theirs).astype(BF16)
    gc_in.append(remote(g_src.at[1 - zh], g_core.at[1 - zh], S_GC2, sibling))
    mine = d3[core]
    g_mine[zh] = dot_nn(ft_ref[...], mine)
    g_mine[1 - zh] = dot_nn(fcross[...], mine)

    for copy in ty_in:
        copy.wait_recv()
    t_z[zi] = (t_y[0] + t_y[1]) + (t_y[2] + t_y[3])
    tz_in = [remote(t_z.at[zi], t_z.at[zi], S_TZ + k - 1, at_z(k)) for k in range(1, 8)]

    for copy in gc_in:
        copy.wait_recv()
    g_c[...] = (g_mine[...] + g_core[...].astype(F32)).astype(BF16)
    gy_in = []
    for k in (1, 2, 3):
        there = (y + k) % 4
        gy_in.append(
            remote(g_c.at[:, pl.ds(48 * there, 48)], g_y.at[y], S_GY + k - 1, at_y(k))
        )
    g_y[y] = g_c[:, pl.ds(48 * y, 48), :]

    for copy in tz_in:
        copy.wait_recv()
    total = t_z[0]
    for k in range(1, 8):
        total = total + t_z[k]
    t_x[x] = total
    tx_in = [remote(t_x.at[x], t_x.at[x], S_TX + k - 1, at_x(k)) for k in (1, 2, 3)]

    for copy in gy_in:
        copy.wait_recv()
    piece = g_y[0].astype(F32)
    for k in (1, 2, 3):
        piece = piece + g_y[k].astype(F32)
    g_zs[...] = piece.astype(BF16)
    gz_in = []
    for k in (4, 3, 5, 2, 6, 1, 7):
        there = (zi + k) % 8
        gz_in.append(remote(g_zs.at[there // 4], g_z.at[zi], S_GZ + k - 1, at_z(k)))
    g_z[zi] = g_zs[zh]

    for copy in tx_in:
        copy.wait_recv()
    table_out[...] = (t_x[0] + t_x[1]) + (t_x[2] + t_x[3])

    for copy in gz_in:
        copy.wait_recv()
    piece = g_z[0].astype(F32)
    for k in range(1, 8):
        piece = piece + g_z[k].astype(F32)
    g_oy[y] = piece.astype(BF16)
    oy_in = [remote(g_oy.at[y], g_oy.at[y], S_OY + k - 1, at_y(k)) for k in (1, 2, 3)]
    for copy in oy_in:
        copy.wait_recv()
    oc_in = remote(g_oy, g_oc, S_OC, sibling)
    oc_in.wait_recv()
    grad_out[core] = g_oy[...]
    grad_out[1 - core] = g_oc[...]
    for copy in sends:
        copy.wait_send()


def finish(att_ref, pieces_ref, table_ref, att_out, grad_out, table_out):
    att_out[0] = att_ref[...]
    for k in range(2):
        for n in range(4):
            grad_out[48 * n : 48 * n + 48, 384 * k : 384 * k + 384] = pieces_ref[k, n].astype(F32)
    for h in range(2):
        table_out[:, h, :] = table_ref[:, 32 * h : 32 * h + 32]


def local(features, w_qkv, buckets, cell_ids, bias_table, d_attended):
    types, levels, _ = bias_table.shape
    vmem = pl.BlockSpec(memory_space=pltpu.VMEM)
    hbm = pl.BlockSpec(memory_space=pl.ANY)
    smem = pl.BlockSpec(memory_space=pltpu.SMEM)
    scratch = [
        pltpu.VMEM((192, 256), BF16),
        pltpu.VMEM((4, 96, 128), BF16),
        pltpu.VMEM((256, 256), BF16),
        pltpu.VMEM((32, 2, 32), F32),
        pltpu.VMEM((8, 128), F32),
        pltpu.VMEM((2, TPAD, 128), F32),
        pltpu.VMEM((4, TPAD, 128), F32),
        pltpu.VMEM((1536, 768), BF16),
        pltpu.VMEM((8, 96, 128), BF16),
        pltpu.VMEM((192, 256), BF16),
        pltpu.VMEM((4, 128, 128), BF16),
        pltpu.VMEM((4, 128, 128), BF16),
        pltpu.VMEM((4, TPAD, 128), F32),
        pltpu.VMEM((2, 64, 256), BF16),
        pltpu.VMEM((2, 64, 128), BF16),
        pltpu.VMEM((128, 128), BF16),
        pltpu.VMEM((18, 128, 256), BF16),
        pltpu.VMEM((NWIN, 128, 128), BF16),
        pltpu.VMEM((NWIN, 128, 128), F32),
        pltpu.VMEM((TPAD, 128), F32),
        pltpu.VMEM((TPAD, 128), F32),
        pltpu.VMEM((4, TPAD, 128), F32),
        pltpu.VMEM((4, TPAD, 128), F32),
        pltpu.VMEM((4, 128, 128), F32),
        pltpu.VMEM((4, 128, 128), BF16),
        pltpu.VMEM((4, 128, 128), BF16),
        pltpu.VMEM((4, TPAD, 128), F32),
        pltpu.VMEM((4, TPAD, 128), F32),
        pltpu.VMEM((18, 128, 256), BF16),
        pltpu.VMEM((6, 2, 128, 256), BF16),
        pltpu.VMEM((2, 2, 128, 256), BF16),
        pltpu.VMEM((2, 2, 128, 256), BF16),
        pltpu.VMEM((2, 2, 128, 256), BF16),
        pltpu.VMEM((2, 2, 128, 256), BF16),
        pltpu.VMEM((4, 2, 128, 256), BF16),
        pltpu.VMEM((4, 128, 128), BF16),
        pltpu.VMEM((2, 256, 384), BF16),
        pltpu.VMEM((2, 192, 384), BF16),
        pltpu.VMEM((2, 192, 384), F32),
        pltpu.VMEM((2, 192, 384), BF16),
        pltpu.VMEM((2, 192, 384), BF16),
        pltpu.VMEM((4, 2, 48, 384), BF16),
        pltpu.VMEM((2, 48, 384), BF16),
        pltpu.VMEM((8, 48, 384), BF16),
        pltpu.VMEM((4, 48, 384), BF16),
        pltpu.VMEM((4, 48, 384), BF16),
        pltpu.VMEM((2, 32, 128), F32),
        pltpu.VMEM((4, 32, 128), F32),
        pltpu.VMEM((8, 32, 128), F32),
        pltpu.VMEM((4, 32, 128), F32),
        pltpu.SemaphoreType.DMA((4,)),
        pltpu.SemaphoreType.DMA((N_SEM,)),
        pltpu.SemaphoreType.DMA((N_SEM,)),
    ]
    att, grad, table = pl.pallas_call(
        kernel,
        out_shape=(
            jax.ShapeDtypeStruct((256, 256), BF16),
            jax.ShapeDtypeStruct((2, 4, 48, 384), BF16),
            jax.ShapeDtypeStruct((types, 128), F32),
        ),
        in_specs=[hbm, hbm, smem, smem, hbm, hbm],
        out_specs=(vmem, vmem, vmem),
        scratch_shapes=scratch,
        compiler_params=pltpu.CompilerParams(collective_id=0, has_side_effects=True),
    )(features.T, w_qkv, buckets, cell_ids, bias_table.transpose(0, 2, 1), d_attended)
    att, grad, table = pl.pallas_call(
        finish,
        out_shape=(
            jax.ShapeDtypeStruct((1, 256, 256), BF16),
            jax.ShapeDtypeStruct((192, 768), F32),
            jax.ShapeDtypeStruct((types, HEADS, levels), F32),
        ),
        in_specs=[vmem] * 3,
        out_specs=(vmem,) * 3,
    )(att, grad, table)
    return (att, grad, table.transpose(0, 2, 1))


def solution(mesh):
    in_specs = (
        P("seq", "cell"),
        P(),
        P("cell", "seq", None),
        P("cell"),
        P(),
        P("cell", "seq", None),
    )
    out_specs = (P("cell", "seq", None), P("cell", None), P())
    return jax.shard_map(local, mesh=mesh, in_specs=in_specs, out_specs=out_specs, check_vma=False)
```

```python
import math

import jax
import jax.numpy as jnp
from jax import lax
from jax.experimental import pallas as pl
from jax.experimental.pallas import tpu as pltpu
from jax.sharding import PartitionSpec as P

HEADS = 2
HD = 128
TILE = 128
BT = 16
NSEQ = 32
NWIN = 17
TPAD = 24
NEG = -1e30
FACTOR = 1.0 / math.sqrt(HD)
F32 = jnp.float32
BF16 = jnp.bfloat16

S_FEAT = 0
S_FCROSS = 7
S_DO = 8
S_BIAS = 11
S_KV = 14
S_Q = 17
S_NEAR = 18
S_FAR = 22
S_ATT = 26
S_TT = 29
S_DKV = 32
S_XKV = 40
S_XQ = 43
S_GC = 46
S_TC = 47
S_GY = 48
S_TY = 51
S_GZ = 54
S_TZ = 61
S_TX = 68
S_OY = 71
S_OC = 74
S_SIB = 75
S_GC2 = 83
S_XKV2 = 84
S_DNEAR = 87
S_DFAR = 91
S_FWD = 95
S_GY2 = 98
S_OC2 = 101
S_TCROSS = 104
N_SEM = 105

CHIP_STEPS = (-2, 2)


def dot_nn(a, b):
    return lax.dot_general(a, b, (((1,), (0,)), ((), ())), preferred_element_type=F32)


def dot_nt(a, b):
    return lax.dot_general(a, b, (((1,), (1,)), ((), ())), preferred_element_type=F32)


def dot_tn(a, b):
    return lax.dot_general(a, b, (((0,), (0,)), ((), ())), preferred_element_type=F32)


class Copy:
    def __init__(self, copy, sends, receives):
        self.copy = copy
        self.sends = sends
        self.receives = receives
        if sends is None:
            copy.start()
        else:
            pl.when(sends)(copy.start)

    def wait_recv(self):
        if self.receives is None:
            self.copy.wait_recv()
        else:
            pl.when(self.receives)(self.copy.wait_recv)

    def wait_send(self):
        if self.sends is None:
            self.copy.wait_send()
        else:
            pl.when(self.sends)(self.copy.wait_send)


def kernel(
    ft_hbm, w_hbm, buckets_ref, ids_ref, tbl_hbm, dout_hbm,
    att_out, grad_out, table_out,
    ft_ref, feat_ref, dout_ref, tbl_ref, row_buf, oh_buf, bias_ref, w_ref, fbuf, fcross, dot_src, dot_buf, bias_buf, proj_kv, proj_q, q_buf, kvw,
    e0_buf, o_buf, m_buf, l_buf, d_buf, w_buf, dof_buf,
    att_src, att_buf, tt_src, tt_buf, dkvw, mate_dkv, far_src, far_in, near_src, near_in, dkv_x, dq_x, d3,
    g_src, g_core, g_c, g_y, g_zs, g_z, g_oy, g_oc,
    t_c, t_y, t_z, t_x, in_sem, send_sem, recv_sem,
):
    cell = lax.axis_index("cell")
    seq = lax.axis_index("seq")
    zh = cell // 4
    x = cell % 4
    z_lo = seq // 8
    y = (seq // 2) % 4
    core = seq % 2
    zi = zh * 4 + z_lo
    head = x % 2
    half = x // 2

    def at_x(k):
        return (zh * 4 + (x + k) % 4, seq)

    def at_cross(k):
        return ((1 - zh) * 4 + (x + k) % 4, seq)

    antipode = at_cross(0)

    def at_far(j):
        return ((1 - zh) * 4 + x, ((z_lo + j) % 4) * 8 + y * 2 + core)

    def at_near(j):
        return (cell, ((z_lo + j) % 4) * 8 + y * 2 + core)

    def at_seq(o):
        return (cell, (seq + o + NSEQ) % NSEQ)

    def at_y(k):
        return (cell, z_lo * 8 + ((y + k) % 4) * 2 + core)

    sibling = (cell, seq + 1 - 2 * core)

    ft_copy = pltpu.make_async_copy(ft_hbm, ft_ref, in_sem.at[0])
    ft_copy.start()
    barrier = pltpu.get_barrier_semaphore()
    greet = [at_cross(k) for k in range(4)] + [at_x(k) for k in (1, 2, 3)]
    greet += [sibling]
    greet += [at_y(k) for k in (1, 2, 3)] + [at_near(j) for j in (1, 2, 3)]
    greet += [at_far(j) for j in (1, 2, 3)]
    for peer in greet:
        pl.semaphore_signal(barrier, inc=1, device_id=peer, device_id_type=pl.DeviceIdType.MESH)
    chip = seq // 2

    def chip_in(d):
        return (chip + d >= 0) & (chip + d < NSEQ // 2)

    def seq_in(o):
        return (seq + o >= 0) & (seq + o < NSEQ)

    expected = len(greet)
    for o in CHIP_STEPS:
        @pl.when(seq_in(o))
        def _():
            pl.semaphore_signal(
                barrier, inc=1, device_id=at_seq(o), device_id_type=pl.DeviceIdType.MESH
            )

        expected = expected + seq_in(o).astype(jnp.int32)

    sends = []

    def remote(src, dst, slot, peer, if_send=None, if_recv=None):
        copy = pltpu.make_async_remote_copy(
            src_ref=src,
            dst_ref=dst,
            send_sem=send_sem.at[slot],
            recv_sem=recv_sem.at[slot],
            device_id=peer,
            device_id_type=pl.DeviceIdType.MESH,
        )
        copy = Copy(copy, if_send, if_recv)
        sends.append(copy)
        return copy

    dout_copy = pltpu.make_async_copy(dout_hbm.at[0], dout_ref, in_sem.at[1])
    dout_copy.start()
    tbl_copy = pltpu.make_async_copy(tbl_hbm, tbl_ref, in_sem.at[2])
    tbl_copy.start()
    w_copy = pltpu.make_async_copy(w_hbm, w_ref, in_sem.at[3])
    w_copy.start()
    ft_copy.wait()
    feat = ft_ref[...].astype(F32).T.astype(BF16)
    for n in range(4):
        rows = feat[64 * n : 64 * n + 64]
        feat_ref[n, 0:64, :] = rows[:, 0:128]
        feat_ref[n, 64:96, 0:64] = rows[0:32, 128:192]
        feat_ref[n, 64:96, 64:128] = rows[32:64, 128:192]
    pl.semaphore_wait(barrier, expected)

    feat_in = {}
    for k in (2, 1, 3, 0):
        there = (x + k) % 4
        feat_in[1, k] = remote(feat_ref.at[there], fbuf.at[cell], S_FEAT + k, at_cross(k))
    for k in (1, 3, 2):
        there = (x + k) % 4
        feat_in[0, k] = remote(feat_ref.at[there], fbuf.at[cell], S_FEAT + 3 + k, at_x(k))
    dout_copy.wait()
    for piece in range(4):
        r, h = piece // 2, piece % 2
        block = dout_ref[128 * r : 128 * r + 128, 128 * h : 128 * h + 128]
        dot_src[piece] = block.astype(F32).T.astype(BF16)
    lane = lax.broadcasted_iota(jnp.int32, (1, 128), 1)
    oh_buf[...] = jnp.zeros((2, TPAD, 128), F32)
    row_buf[...] = jnp.zeros((8, 128), F32)
    for r in range(2):
        for o in range(BT):
            oh_buf[r, r + o : r + o + 1, :] = (lane == buckets_ref[0, r, o]).astype(F32)
    tbl_copy.wait()
    hit = (lax.broadcasted_iota(jnp.int32, (32, 128), 0) == ids_ref[0]).astype(F32)
    tile_at = lax.broadcasted_iota(jnp.int32, (TPAD, 128), 0)
    global_tile = 2 * seq - 8 + tile_at
    in_range = (global_tile >= 0) & (global_tile < 2 * NSEQ)
    for h in range(2):
        row_buf[h : h + 1, 0:32] = jnp.sum(
            jnp.where(hit[:, 0:32] > 0.0, tbl_ref[:, h, :], 0.0), axis=0, keepdims=True
        )
        for r in range(2):
            level = jnp.sum(oh_buf[r] * row_buf[h : h + 1, :], axis=1, keepdims=True)
            valid = in_range & (tile_at >= r) & (tile_at < r + BT)
            bias_ref[2 * r + h] = jnp.where(valid, jnp.broadcast_to(level, (TPAD, 128)), NEG)

    do_in = []
    bias_in = []
    for k in (1, 2, 3):
        there = (x + k) % 4
        do_in.append(remote(dot_src.at[there], dot_buf.at[x], S_DO + k - 1, at_x(k)))
        bias_in.append(remote(bias_ref.at[there], bias_buf.at[x], S_BIAS + k - 1, at_x(k)))
    cross_in = remote(ft_ref, fcross, S_FCROSS, antipode)

    dot_buf[x] = dot_src[x]
    bias_buf[x] = bias_ref[x]
    fbuf[cell] = feat_ref[x]
    for t in range(18):
        tile = 2 * seq - 8 + t

        @pl.when((tile < 0) | (tile >= 2 * NSEQ))
        def _():
            kvw[t] = jnp.zeros((128, 256), BF16)

    w_copy.wait()

    zero_tile = jnp.zeros((2, 128, 256), BF16)
    dkvw[17] = jnp.zeros((128, 256), BF16)
    mate_dkv[0] = zero_tile
    mate_dkv[5] = zero_tile
    for n, d in enumerate((1, -1)):
        @pl.when(jnp.logical_not(chip_in(d)))
        def _():
            far_in[n] = zero_tile
            near_in[n] = zero_tile

    def project(c, rows):
        low = pl.multiple_of(192 * c, 64)
        tail = jnp.concatenate([rows[64:96, 0:64], rows[64:96, 64:128]], axis=0)
        return dot_nn(rows[0:64], w_ref[pl.ds(low, 128), :]) + dot_nn(
            tail, w_ref[pl.ds(pl.multiple_of(low + 128, 64), 64), :]
        )

    proj = project(cell, fbuf[cell])
    for k in (1, 3, 2):
        feat_in[0, k].wait_recv()
        c = zh * 4 + (x - k + 4) % 4
        proj = proj + project(c, fbuf[c])
    for k in (2, 1, 3, 0):
        feat_in[1, k].wait_recv()
        c = (1 - zh) * 4 + (x - k + 4) % 4
        proj = proj + project(c, fbuf[c])
    projected = proj.astype(BF16)
    for h in range(2):
        proj_q[h] = projected[:, 128 * h : 128 * h + 128]
        proj_kv[h, :, 0:128] = projected[:, 256 + 128 * h : 384 + 128 * h]
        proj_kv[h, :, 128:256] = projected[:, 512 + 128 * h : 640 + 128 * h]

    my_tile = 8 + x // 2
    my_rows = pl.ds(64 * (x % 2), 64)
    kv_in = []
    for k in (1, 2, 3):
        there = (x + k) % 4
        kv_in.append(
            remote(proj_kv.at[there % 2], kvw.at[my_tile, my_rows], S_KV + k - 1, at_x(k))
        )
    mate = (zh * 4 + x + 1 - 2 * (x % 2), seq)
    q_in = remote(proj_q.at[1 - head], q_buf.at[my_rows], S_Q, mate)
    kvw[my_tile, my_rows] = proj_kv[head]
    q_buf[my_rows] = proj_q[head]
    for copy in kv_in:
        copy.wait_recv()

    def relay(src_tile, dst_tile, slot, if_send=None, if_recv=None):
        return remote(
            kvw.at[src_tile], kvw.at[dst_tile], slot, sibling, if_send, if_recv
        )

    near = {}
    far = {}
    mate_in = {}
    pairs = [(t, d) for t in range(2) for d in (-1, 1)]
    for n, (t, d) in enumerate(pairs):
        near[-d, t] = remote(
            kvw.at[8 + t],
            kvw.at[8 - 4 * d + t],
            S_NEAR + n,
            at_seq(2 * d),
            chip_in(d),
            chip_in(-d),
        )
    for t in range(2):
        mate_in[0, t] = relay(8 + t, 6 + 4 * core + t, S_SIB + t)

    def pass_on(t):
        for d in (-1, 1):
            near[d, t].wait_recv()
            here = 8 + 4 * d + t
            n = pairs.index((t, d))
            far[2 * d, t] = remote(
                kvw.at[here],
                kvw.at[8 + 8 * d + t],
                S_FAR + n,
                at_seq(-2 * d),
                chip_in(d) & chip_in(-d),
                chip_in(2 * d),
            )
            mate_in[d, t] = relay(
                here, 6 + 4 * d + 4 * core + t, S_SIB + 2 + n, chip_in(d), chip_in(d)
            )

    def pass_far(t):
        for d in (-2, 2):
            far[d, t].wait_recv()
        mate_in[2, t] = relay(
            16 - 16 * core + t,
            14 - 12 * core + t,
            S_SIB + 6 + t,
            chip_in(2 - 4 * core),
            chip_in(4 * core - 2),
        )

    q_in.wait_recv()
    for copy in do_in + bias_in:
        copy.wait_recv()

    q_tile = q_buf[...]
    for c in range(4):
        dof_buf[c] = dot_buf[c].astype(F32)
    m_buf[...] = jnp.zeros((TPAD, 128), F32)
    l_buf[...] = jnp.zeros((TPAD, 128), F32)
    d_buf[...] = jnp.zeros((4, TPAD, 128), F32)

    def forward_tile(t):
        keys = kvw[t, :, 0:128]
        values = kvw[t, :, 128:256]
        s = dot_nt(keys, q_tile) * FACTOR
        top = jnp.max(s, axis=0, keepdims=True)
        e0 = jnp.exp(s - top)
        m_buf[pl.ds(t, 1), :] = top
        l_buf[pl.ds(t, 1), :] = jnp.sum(e0, axis=0, keepdims=True)
        e0b = e0.astype(BF16)
        e0_buf[t] = e0b
        o_t = dot_tn(values, e0b)
        o_buf[t] = o_t
        for c in range(4):
            d_buf[c, pl.ds(t, 1), :] = jnp.sum(dof_buf[c] * o_t, axis=0, keepdims=True)

    forward_tile(8)
    pass_on(0)
    forward_tile(9)
    pass_on(1)
    for t in range(2):
        mate_in[0, t].wait_recv()
        forward_tile(10 - 4 * core + t)
    for t in range(2):
        for d in (-1, 1):
            forward_tile(8 + 4 * d + t)
    pass_far(0)
    for t in range(2):
        for d in (-1, 1):
            mate_in[d, t].wait_recv()
            forward_tile(10 + 4 * d - 4 * core + t)
    pass_far(1)
    forward_tile(0)
    forward_tile(1)
    forward_tile(16)
    for t in range(2):
        mate_in[2, t].wait_recv()
        forward_tile(2 + 12 * core + t)

    m_all = m_buf[...]
    l_all = l_buf[...]
    big = jnp.zeros((TPAD, 128), F32)
    tt_in = []
    for c in range(4):
        z = m_all + bias_buf[c]
        top = jnp.max(z, axis=0, keepdims=True)
        ex = jnp.exp(z - top)
        mass = jnp.sum(ex * l_all, axis=0, keepdims=True)
        w_c = ex / mass
        w_buf[c] = w_c
        delta = jnp.sum(w_c * d_buf[c], axis=0, keepdims=True)
        big = big + w_c * delta
        tt_src[c] = w_c * (d_buf[c] - delta * l_all)
    for k in (1, 2, 3):
        there = (x + k) % 4
        tt_in.append(remote(tt_src.at[there], tt_buf.at[x], S_TT + k - 1, at_x(k)))
    tt_buf[x] = tt_src[x]

    dq_acc = jnp.zeros((128, 128), F32)

    def backward_slot(slot, dq_acc):
        for t in (2 * slot, 2 * slot + 1):
            if t >= NWIN:
                continue
            g_t = w_buf[0, t : t + 1, :] * dof_buf[0]
            for c in (1, 2, 3):
                g_t = g_t + w_buf[c, t : t + 1, :] * dof_buf[c]
            gb = g_t.astype(BF16)
            e0b = e0_buf[t]
            dp = dot_nn(kvw[t, :, 128:256], gb)
            ds = (e0b.astype(F32) * (dp - big[t : t + 1, :])).astype(BF16)
            dkvw[t, :, 0:128] = (dot_nn(ds, q_tile) * FACTOR).astype(BF16)
            dkvw[t, :, 128:256] = dot_nt(e0b, gb).astype(BF16)
            dq_acc = dq_acc + dot_tn(ds, kvw[t, :, 0:128])
        return dq_acc

    mate_in = {}
    for slot in (1, 7, 3, 5):
        dq_acc = backward_slot(slot, dq_acc)
        j = slot // 2
        mate_in[j] = remote(
            dkvw.at[pl.ds(2 * slot, 2)], mate_dkv.at[j + 1], S_DKV + j, sibling
        )

    def chip_sum(e, t):
        return dkvw[4 * e + t].astype(F32) + mate_dkv[e + core, t].astype(F32)

    dq_acc = backward_slot(0, dq_acc)
    dq_acc = backward_slot(8, dq_acc)
    mate_in[0].wait_recv()
    mate_in[3].wait_recv()
    far = {}
    for t in range(2):
        for n, (e, d) in enumerate(((0, -1), (4, 1))):
            far_src[n, t] = chip_sum(e, t).astype(BF16)
            far[n, t] = remote(
                far_src.at[n, t],
                far_in.at[n, t],
                S_DFAR + 2 * t + n,
                at_seq(2 * d),
                chip_in(2 * d),
                chip_in(1) & chip_in(-1),
            )
    for slot in (2, 6, 4):
        dq_acc = backward_slot(slot, dq_acc)
    dq_x[x] = (dq_acc * FACTOR).astype(BF16)
    xq_in = [remote(dq_x.at[x], dq_x.at[x], S_XQ + k - 1, at_x(k)) for k in (1, 2, 3)]

    mate_in[1].wait_recv()
    mate_in[2].wait_recv()
    near = {}
    for t in range(2):
        for n, (e, d) in enumerate(((1, -1), (3, 1))):
            far[n, t].wait_recv()
            near_src[n, t] = (chip_sum(e, t) + far_in[n, t].astype(F32)).astype(BF16)
            near[n, t] = remote(
                near_src.at[n, t],
                near_in.at[n, t],
                S_DNEAR + 2 * t + n,
                at_seq(2 * d),
                chip_in(d),
                chip_in(-d),
            )

    for c in range(4):
        acc = jnp.zeros((128, 128), F32)
        for t in range(NWIN):
            acc = acc + w_buf[c, t : t + 1, :] * o_buf[t]
        att_src[c] = acc.T.astype(BF16)

    xkv_in = []
    for t in range(2):
        for n in range(2):
            near[n, t].wait_recv()
        acc = chip_sum(2, t) + near_in[0, t].astype(F32) + near_in[1, t].astype(F32)
        dkv_x[x, t] = acc.astype(BF16)
        xkv_in.append(
            [
                remote(
                    dkv_x.at[x, t], dkv_x.at[x, t], (S_XKV, S_XKV2)[t] + k - 1, at_x(k)
                )
                for k in (1, 2, 3)
            ]
        )

    for copy in tt_in:
        copy.wait_recv()
    ones = jnp.ones((8, 128), F32)
    rows = []
    for h in range(2):
        row = jnp.zeros((8, 128), F32)
        for r in range(2):
            sums = lax.dot_general(
                ones, tt_buf[2 * r + h], (((1,), (1,)), ((), ())),
                precision=lax.Precision.HIGHEST, preferred_element_type=F32,
            )
            row = row + lax.dot_general(
                sums, oh_buf[r], (((1,), (0,)), ((), ())),
                precision=lax.Precision.HIGHEST, preferred_element_type=F32,
            )
        rows.append(row)
    both_heads = rows[0] + pltpu.roll(rows[1], 32, axis=1)
    t_c[core] = both_heads
    tc_in = remote(t_c.at[core], t_c.at[core], S_TC, sibling)

    for copy in xq_in:
        copy.wait_recv()
    for t in range(2):
        for copy in xkv_in[t]:
            copy.wait_recv()
        at_rows = slice(128 * t, 128 * t + 128)
        for h in range(2):
            d3[0, at_rows, 128 * h : 128 * h + 128] = dq_x[2 * t + h]
            both = dkv_x[h, t].astype(F32) + dkv_x[2 + h, t].astype(F32)
            bothb = both.astype(BF16)
            d3[h, at_rows, 256 - 256 * h : 384 - 256 * h] = bothb[:, 0:128]
            d3[1, at_rows, 128 + 128 * h : 256 + 128 * h] = bothb[:, 128:256]

    att_in = []
    for k in (1, 2, 3):
        there = (x + k) % 4
        att_in.append(remote(att_src.at[there], att_buf.at[x], S_ATT + k - 1, at_x(k)))
    att_buf[x] = att_src[x]

    tc_in.wait_recv()
    t_y[y] = t_c[0] + t_c[1]
    ty_in = [remote(t_y.at[y], t_y.at[y], S_TY + k - 1, at_y(k)) for k in (1, 2, 3)]

    cross_in.wait_recv()
    halves = ((1 - zh, fcross, S_GC, S_GY), (zh, ft_ref, S_GC2, S_GY2))
    theirs = d3[1 - core]
    gc_in = []
    for part, rows_ref, slot, _ in halves:
        g_src[part] = dot_nn(rows_ref[...], theirs).astype(BF16)
        gc_in.append(remote(g_src.at[part], g_core.at[part], slot, sibling))
    mine = d3[core]
    gy_in = []
    for n, (part, rows_ref, _, slot) in enumerate(halves):
        product = dot_nn(rows_ref[...], mine)
        gc_in[n].wait_recv()
        g_c[part] = (product + g_core[part].astype(F32)).astype(BF16)
        for k in (1, 2, 3):
            there = (y + k) % 4
            gy_in.append(
                remote(
                    g_c.at[part, pl.ds(48 * there, 48)],
                    g_y.at[y, part],
                    slot + k - 1,
                    at_y(k),
                )
            )
        g_y[y, part] = g_c[part, pl.ds(48 * y, 48), :]

    for copy in ty_in:
        copy.wait_recv()
    t_z[z_lo] = (t_y[0] + t_y[1]) + (t_y[2] + t_y[3])
    tz_in = [
        remote(t_z.at[z_lo], t_z.at[z_lo], S_TZ + j - 1, at_near(j)) for j in (1, 2, 3)
    ]
    gz_in = []
    for n, (part, _, _, _) in enumerate(halves):
        for copy in gy_in[3 * n : 3 * n + 3]:
            copy.wait_recv()
        piece = g_y[0, part].astype(F32)
        for k in (1, 2, 3):
            piece = piece + g_y[k, part].astype(F32)
        g_zs[part] = piece.astype(BF16)
        for j in (0, 1, 3, 2) if n == 0 else (2, 1, 3):
            peer = at_far(j) if n == 0 else at_near(j)
            slot = S_GZ + j if n == 0 else S_GZ + 3 + j
            gz_in.append(remote(g_zs.at[part], g_z.at[zi], slot, peer))
    g_z[zi] = g_zs[zh]

    for copy in tz_in:
        copy.wait_recv()
    sums = ((t_z[0] + t_z[1]) + (t_z[2] + t_z[3]))[0:1, :]
    at_row = lax.broadcasted_iota(jnp.int32, (8, 128), 0)
    at_type = (lax.broadcasted_iota(jnp.int32, (8, 128), 1) == ids_ref[0]).astype(F32)
    t_x[zh, x] = jnp.where(at_row == 0, sums, jnp.where(at_row == 1, at_type, 0.0))
    tx_in = [remote(t_x.at[zh, x], t_x.at[zh, x], S_TX + k - 1, at_x(k)) for k in (1, 2, 3)]

    for copy in tx_in:
        copy.wait_recv()
    tcross_in = remote(t_x.at[zh], t_x.at[zh], S_TCROSS, antipode)

    for copy in gz_in:
        copy.wait_recv()
    piece = g_z[0].astype(F32)
    for k in range(1, 8):
        piece = piece + g_z[k].astype(F32)
    g_oy[y] = piece.astype(BF16)
    oy_in = [remote(g_oy.at[y], g_oy.at[y], S_OY + k - 1, at_y(k)) for k in (1, 2, 3)]
    oc_in = [remote(g_oy.at[y], g_oc.at[y], S_OC, sibling)]
    for copy in att_in:
        copy.wait_recv()
    for piece in range(4):
        r, h = piece // 2, piece % 2
        att_out[128 * r : 128 * r + 128, 128 * h : 128 * h + 128] = att_buf[piece]

    tcross_in.wait_recv()
    cells = [t_x[c // 4, c % 4] for c in range(8)]
    total = lax.dot_general(
        jnp.concatenate([tile[1:2] for tile in cells], axis=0),
        jnp.concatenate([tile[0:1] for tile in cells], axis=0),
        (((0,), (0,)), ((), ())),
        precision=lax.Precision.HIGHEST, preferred_element_type=F32,
    )
    table_out[...] = total[0:32]
    for k in (1, 3, 2):
        source = (y - k + 4) % 4
        oy_in[k - 1].wait_recv()
        oc_in.append(remote(g_oy.at[source], g_oc.at[source], S_OC2 + k - 1, sibling))
    for copy in oc_in:
        copy.wait_recv()
    grad_out[core] = g_oy[...]
    grad_out[1 - core] = g_oc[...]
    for copy in sends:
        copy.wait_send()


def finish(att_ref, pieces_ref, table_ref, att_out, grad_out, table_out):
    att_out[0] = att_ref[...]
    for k in range(2):
        for n in range(4):
            grad_out[48 * n : 48 * n + 48, 384 * k : 384 * k + 384] = pieces_ref[k, n].astype(F32)
    for h in range(2):
        table_out[:, h, :] = table_ref[:, 32 * h : 32 * h + 32]


def local(features, w_qkv, buckets, cell_ids, bias_table, d_attended):
    types, levels, _ = bias_table.shape
    vmem = pl.BlockSpec(memory_space=pltpu.VMEM)
    hbm = pl.BlockSpec(memory_space=pl.ANY)
    smem = pl.BlockSpec(memory_space=pltpu.SMEM)
    scratch = [
        pltpu.VMEM((192, 256), BF16),
        pltpu.VMEM((4, 96, 128), BF16),
        pltpu.VMEM((256, 256), BF16),
        pltpu.VMEM((32, 2, 32), F32),
        pltpu.VMEM((8, 128), F32),
        pltpu.VMEM((2, TPAD, 128), F32),
        pltpu.VMEM((4, TPAD, 128), F32),
        pltpu.VMEM((1536, 768), BF16),
        pltpu.VMEM((8, 96, 128), BF16),
        pltpu.VMEM((192, 256), BF16),
        pltpu.VMEM((4, 128, 128), BF16),
        pltpu.VMEM((4, 128, 128), BF16),
        pltpu.VMEM((4, TPAD, 128), F32),
        pltpu.VMEM((2, 64, 256), BF16),
        pltpu.VMEM((2, 64, 128), BF16),
        pltpu.VMEM((128, 128), BF16),
        pltpu.VMEM((18, 128, 256), BF16),
        pltpu.VMEM((NWIN, 128, 128), BF16),
        pltpu.VMEM((NWIN, 128, 128), F32),
        pltpu.VMEM((TPAD, 128), F32),
        pltpu.VMEM((TPAD, 128), F32),
        pltpu.VMEM((4, TPAD, 128), F32),
        pltpu.VMEM((4, TPAD, 128), F32),
        pltpu.VMEM((4, 128, 128), F32),
        pltpu.VMEM((4, 128, 128), BF16),
        pltpu.VMEM((4, 128, 128), BF16),
        pltpu.VMEM((4, TPAD, 128), F32),
        pltpu.VMEM((4, TPAD, 128), F32),
        pltpu.VMEM((18, 128, 256), BF16),
        pltpu.VMEM((6, 2, 128, 256), BF16),
        pltpu.VMEM((2, 2, 128, 256), BF16),
        pltpu.VMEM((2, 2, 128, 256), BF16),
        pltpu.VMEM((2, 2, 128, 256), BF16),
        pltpu.VMEM((2, 2, 128, 256), BF16),
        pltpu.VMEM((4, 2, 128, 256), BF16),
        pltpu.VMEM((4, 128, 128), BF16),
        pltpu.VMEM((2, 256, 384), BF16),
        pltpu.VMEM((2, 192, 384), BF16),
        pltpu.VMEM((2, 192, 384), BF16),
        pltpu.VMEM((2, 192, 384), BF16),
        pltpu.VMEM((4, 2, 48, 384), BF16),
        pltpu.VMEM((2, 48, 384), BF16),
        pltpu.VMEM((8, 48, 384), BF16),
        pltpu.VMEM((4, 48, 384), BF16),
        pltpu.VMEM((4, 48, 384), BF16),
        pltpu.VMEM((2, 8, 128), F32),
        pltpu.VMEM((4, 8, 128), F32),
        pltpu.VMEM((4, 8, 128), F32),
        pltpu.VMEM((2, 4, 8, 128), F32),
        pltpu.SemaphoreType.DMA((4,)),
        pltpu.SemaphoreType.DMA((N_SEM,)),
        pltpu.SemaphoreType.DMA((N_SEM,)),
    ]
    att, grad, table = pl.pallas_call(
        kernel,
        out_shape=(
            jax.ShapeDtypeStruct((256, 256), BF16),
            jax.ShapeDtypeStruct((2, 4, 48, 384), BF16),
            jax.ShapeDtypeStruct((types, 128), F32),
        ),
        in_specs=[hbm, hbm, smem, smem, hbm, hbm],
        out_specs=(vmem, vmem, vmem),
        scratch_shapes=scratch,
        compiler_params=pltpu.CompilerParams(collective_id=0, has_side_effects=True),
    )(features.T, w_qkv, buckets, cell_ids, bias_table.transpose(0, 2, 1), d_attended)
    att, grad, table = pl.pallas_call(
        finish,
        out_shape=(
            jax.ShapeDtypeStruct((1, 256, 256), BF16),
            jax.ShapeDtypeStruct((192, 768), F32),
            jax.ShapeDtypeStruct((types, HEADS, levels), F32),
        ),
        in_specs=[vmem] * 3,
        out_specs=(vmem,) * 3,
    )(att, grad, table)
    return (att, grad, table.transpose(0, 2, 1))


def solution(mesh):
    in_specs = (
        P("seq", "cell"),
        P(),
        P("cell", "seq", None),
        P("cell"),
        P(),
        P("cell", "seq", None),
    )
    out_specs = (P("cell", "seq", None), P("cell", None), P())
    return jax.shard_map(local, mesh=mesh, in_specs=in_specs, out_specs=out_specs, check_vma=False)
```

```python
import math

import jax
import jax.numpy as jnp
from jax import lax
from jax.experimental import pallas as pl
from jax.experimental.pallas import tpu as pltpu
from jax.sharding import PartitionSpec as P

HEADS = 2
HD = 128
TILE = 128
BT = 16
NSEQ = 32
NWIN = 17
TPAD = 24
NEG = -1e30
FACTOR = 1.0 / math.sqrt(HD)
F32 = jnp.float32
BF16 = jnp.bfloat16

S_FEAT = 0
S_FCROSS = 7
S_DO = 8
S_BIAS = 11
S_KV = 14
S_Q = 17
S_NEAR = 18
S_FAR = 22
S_ATT = 26
S_TT = 29
S_DKV = 32
S_XKV = 40
S_XQ = 43
S_GC = 46
S_TC = 47
S_GY = 48
S_TY = 51
S_GZ = 54
S_TZ = 61
S_TX = 68
S_OY = 71
S_OC = 74
S_SIB = 75
S_GC2 = 83
S_XKV2 = 84
S_DNEAR = 87
S_DFAR = 91
S_FWD = 95
S_GY2 = 98
S_OC2 = 101
S_TCROSS = 104
N_SEM = 105

CHIP_STEPS = (-2, 2)


def dot_nn(a, b):
    return lax.dot_general(a, b, (((1,), (0,)), ((), ())), preferred_element_type=F32)


def dot_nt(a, b):
    return lax.dot_general(a, b, (((1,), (1,)), ((), ())), preferred_element_type=F32)


def dot_tn(a, b):
    return lax.dot_general(a, b, (((0,), (0,)), ((), ())), preferred_element_type=F32)


class Copy:
    def __init__(self, copy, sends, receives):
        self.copy = copy
        self.sends = sends
        self.receives = receives
        if sends is None:
            copy.start()
        else:
            pl.when(sends)(copy.start)

    def wait_recv(self):
        if self.receives is None:
            self.copy.wait_recv()
        else:
            pl.when(self.receives)(self.copy.wait_recv)

    def wait_send(self):
        if self.sends is None:
            self.copy.wait_send()
        else:
            pl.when(self.sends)(self.copy.wait_send)


def kernel(
    ft_hbm, w_hbm, buckets_ref, ids_ref, tbl_hbm, dout_hbm,
    att_out, grad_out, table_out,
    ft_ref, feat_ref, dout_ref, tbl_ref, row_buf, oh_buf, bias_ref, w_ref, fbuf, fcross, dot_src, dot_buf, bias_buf, proj_kv, proj_q, q_buf, kvw,
    e0_buf, o_buf, m_buf, l_buf, d_buf, w_buf, dof_buf,
    att_src, att_buf, tt_src, tt_buf, dkvw, mate_dkv, far_src, far_in, near_src, near_in, dkv_x, dq_x, d3,
    g_src, g_core, g_c, g_y, g_zs, g_z, g_oy, g_oc,
    t_c, t_y, t_z, t_x, in_sem, send_sem, recv_sem,
):
    cell = lax.axis_index("cell")
    seq = lax.axis_index("seq")
    zh = cell // 4
    x = cell % 4
    z_lo = seq // 8
    y = (seq // 2) % 4
    core = seq % 2
    zi = zh * 4 + z_lo
    head = x % 2
    half = x // 2

    def at_x(k):
        return (zh * 4 + (x + k) % 4, seq)

    def at_cross(k):
        return ((1 - zh) * 4 + (x + k) % 4, seq)

    antipode = at_cross(0)

    def at_far(j):
        return ((1 - zh) * 4 + x, ((z_lo + j) % 4) * 8 + y * 2 + core)

    def at_near(j):
        return (cell, ((z_lo + j) % 4) * 8 + y * 2 + core)

    def at_seq(o):
        return (cell, (seq + o + NSEQ) % NSEQ)

    def at_y(k):
        return (cell, z_lo * 8 + ((y + k) % 4) * 2 + core)

    sibling = (cell, seq + 1 - 2 * core)

    ft_copy = pltpu.make_async_copy(ft_hbm, ft_ref, in_sem.at[0])
    ft_copy.start()
    barrier = pltpu.get_barrier_semaphore()
    greet = [at_cross(k) for k in range(4)] + [at_x(k) for k in (1, 2, 3)]
    greet += [sibling]
    greet += [at_y(k) for k in (1, 2, 3)] + [at_near(j) for j in (1, 2, 3)]
    greet += [at_far(j) for j in (1, 2, 3)]
    for peer in greet:
        pl.semaphore_signal(barrier, inc=1, device_id=peer, device_id_type=pl.DeviceIdType.MESH)
    chip = seq // 2

    def chip_in(d):
        return (chip + d >= 0) & (chip + d < NSEQ // 2)

    def seq_in(o):
        return (seq + o >= 0) & (seq + o < NSEQ)

    expected = len(greet)
    for o in CHIP_STEPS:
        @pl.when(seq_in(o))
        def _():
            pl.semaphore_signal(
                barrier, inc=1, device_id=at_seq(o), device_id_type=pl.DeviceIdType.MESH
            )

        expected = expected + seq_in(o).astype(jnp.int32)

    sends = []

    def remote(src, dst, slot, peer, if_send=None, if_recv=None):
        copy = pltpu.make_async_remote_copy(
            src_ref=src,
            dst_ref=dst,
            send_sem=send_sem.at[slot],
            recv_sem=recv_sem.at[slot],
            device_id=peer,
            device_id_type=pl.DeviceIdType.MESH,
        )
        copy = Copy(copy, if_send, if_recv)
        sends.append(copy)
        return copy

    dout_copy = pltpu.make_async_copy(dout_hbm.at[0], dout_ref, in_sem.at[1])
    dout_copy.start()
    tbl_copy = pltpu.make_async_copy(tbl_hbm, tbl_ref, in_sem.at[2])
    tbl_copy.start()
    w_copy = pltpu.make_async_copy(w_hbm, w_ref, in_sem.at[3])
    w_copy.start()
    ft_copy.wait()
    feat = ft_ref[...].astype(F32).T.astype(BF16)
    for n in range(4):
        rows = feat[64 * n : 64 * n + 64]
        feat_ref[n, 0:64, :] = rows[:, 0:128]
        feat_ref[n, 64:96, 0:64] = rows[0:32, 128:192]
        feat_ref[n, 64:96, 64:128] = rows[32:64, 128:192]
    pl.semaphore_wait(barrier, expected)

    feat_in = {}
    for k in (2, 1, 3, 0):
        there = (x + k) % 4
        feat_in[1, k] = remote(feat_ref.at[there], fbuf.at[cell], S_FEAT + k, at_cross(k))
    for k in (1, 3, 2):
        there = (x + k) % 4
        feat_in[0, k] = remote(feat_ref.at[there], fbuf.at[cell], S_FEAT + 3 + k, at_x(k))
    dout_copy.wait()
    for piece in range(4):
        r, h = piece // 2, piece % 2
        block = dout_ref[128 * r : 128 * r + 128, 128 * h : 128 * h + 128]
        dot_src[piece] = block.astype(F32).T.astype(BF16)
    lane = lax.broadcasted_iota(jnp.int32, (1, 128), 1)
    oh_buf[...] = jnp.zeros((2, TPAD, 128), F32)
    row_buf[...] = jnp.zeros((8, 128), F32)
    for r in range(2):
        for o in range(BT):
            oh_buf[r, r + o : r + o + 1, :] = (lane == buckets_ref[0, r, o]).astype(F32)
    tbl_copy.wait()
    hit = (lax.broadcasted_iota(jnp.int32, (32, 128), 0) == ids_ref[0]).astype(F32)
    tile_at = lax.broadcasted_iota(jnp.int32, (TPAD, 128), 0)
    global_tile = 2 * seq - 8 + tile_at
    in_range = (global_tile >= 0) & (global_tile < 2 * NSEQ)
    for h in range(2):
        row_buf[h : h + 1, 0:32] = jnp.sum(
            jnp.where(hit[:, 0:32] > 0.0, tbl_ref[:, h, :], 0.0), axis=0, keepdims=True
        )
        for r in range(2):
            level = jnp.sum(oh_buf[r] * row_buf[h : h + 1, :], axis=1, keepdims=True)
            valid = in_range & (tile_at >= r) & (tile_at < r + BT)
            bias_ref[2 * r + h] = jnp.where(valid, jnp.broadcast_to(level, (TPAD, 128)), NEG)

    do_in = []
    bias_in = []
    for k in (1, 2, 3):
        there = (x + k) % 4
        do_in.append(remote(dot_src.at[there], dot_buf.at[x], S_DO + k - 1, at_x(k)))
        bias_in.append(remote(bias_ref.at[there], bias_buf.at[x], S_BIAS + k - 1, at_x(k)))

    dot_buf[x] = dot_src[x]
    bias_buf[x] = bias_ref[x]
    fbuf[cell] = feat_ref[x]
    for t in range(18):
        tile = 2 * seq - 8 + t

        @pl.when((tile < 0) | (tile >= 2 * NSEQ))
        def _():
            kvw[t] = jnp.zeros((128, 256), BF16)

    w_copy.wait()

    zero_tile = jnp.zeros((2, 128, 256), BF16)
    dkvw[17] = jnp.zeros((128, 256), BF16)
    mate_dkv[0] = zero_tile
    mate_dkv[5] = zero_tile
    for n, d in enumerate((1, -1)):
        @pl.when(jnp.logical_not(chip_in(d)))
        def _():
            far_in[n] = zero_tile
            near_in[n] = zero_tile

    def project(c, rows):
        low = pl.multiple_of(192 * c, 64)
        tail = jnp.concatenate([rows[64:96, 0:64], rows[64:96, 64:128]], axis=0)
        return dot_nn(rows[0:64], w_ref[pl.ds(low, 128), :]) + dot_nn(
            tail, w_ref[pl.ds(pl.multiple_of(low + 128, 64), 64), :]
        )

    proj = project(cell, fbuf[cell])
    for k in (1, 3, 2):
        feat_in[0, k].wait_recv()
        c = zh * 4 + (x - k + 4) % 4
        proj = proj + project(c, fbuf[c])
    for k in (2, 1, 3, 0):
        feat_in[1, k].wait_recv()
        c = (1 - zh) * 4 + (x - k + 4) % 4
        proj = proj + project(c, fbuf[c])
    projected = proj.astype(BF16)
    for h in range(2):
        proj_q[h] = projected[:, 128 * h : 128 * h + 128]
        proj_kv[h, :, 0:128] = projected[:, 256 + 128 * h : 384 + 128 * h]
        proj_kv[h, :, 128:256] = projected[:, 512 + 128 * h : 640 + 128 * h]

    cross_in = remote(ft_ref, fcross, S_FCROSS, antipode)
    my_tile = 8 + x // 2
    my_rows = pl.ds(64 * (x % 2), 64)
    kv_in = []
    for k in (1, 2, 3):
        there = (x + k) % 4
        kv_in.append(
            remote(proj_kv.at[there % 2], kvw.at[my_tile, my_rows], S_KV + k - 1, at_x(k))
        )
    mate = (zh * 4 + x + 1 - 2 * (x % 2), seq)
    q_in = remote(proj_q.at[1 - head], q_buf.at[my_rows], S_Q, mate)
    kvw[my_tile, my_rows] = proj_kv[head]
    q_buf[my_rows] = proj_q[head]
    for copy in kv_in:
        copy.wait_recv()

    def relay(src_tile, dst_tile, slot, if_send=None, if_recv=None):
        return remote(
            kvw.at[src_tile], kvw.at[dst_tile], slot, sibling, if_send, if_recv
        )

    near = {}
    far = {}
    mate_in = {}
    pairs = [(t, d) for t in range(2) for d in (-1, 1)]
    for n, (t, d) in enumerate(pairs):
        near[-d, t] = remote(
            kvw.at[8 + t],
            kvw.at[8 - 4 * d + t],
            S_NEAR + n,
            at_seq(2 * d),
            chip_in(d),
            chip_in(-d),
        )
    for t in range(2):
        mate_in[0, t] = relay(8 + t, 6 + 4 * core + t, S_SIB + t)

    def pass_on(t):
        for d in (-1, 1):
            near[d, t].wait_recv()
            here = 8 + 4 * d + t
            n = pairs.index((t, d))
            far[2 * d, t] = remote(
                kvw.at[here],
                kvw.at[8 + 8 * d + t],
                S_FAR + n,
                at_seq(-2 * d),
                chip_in(d) & chip_in(-d),
                chip_in(2 * d),
            )
            mate_in[d, t] = relay(
                here, 6 + 4 * d + 4 * core + t, S_SIB + 2 + n, chip_in(d), chip_in(d)
            )

    def pass_far(t):
        for d in (-2, 2):
            far[d, t].wait_recv()
        mate_in[2, t] = relay(
            16 - 16 * core + t,
            14 - 12 * core + t,
            S_SIB + 6 + t,
            chip_in(2 - 4 * core),
            chip_in(4 * core - 2),
        )

    q_in.wait_recv()
    for copy in do_in + bias_in:
        copy.wait_recv()

    q_tile = q_buf[...]
    for c in range(4):
        dof_buf[c] = dot_buf[c].astype(F32)
    m_buf[...] = jnp.zeros((TPAD, 128), F32)
    l_buf[...] = jnp.zeros((TPAD, 128), F32)
    d_buf[...] = jnp.zeros((4, TPAD, 128), F32)

    def forward_tile(t):
        keys = kvw[t, :, 0:128]
        values = kvw[t, :, 128:256]
        s = dot_nt(keys, q_tile) * FACTOR
        top = jnp.max(s, axis=0, keepdims=True)
        e0 = jnp.exp(s - top)
        m_buf[pl.ds(t, 1), :] = top
        l_buf[pl.ds(t, 1), :] = jnp.sum(e0, axis=0, keepdims=True)
        e0b = e0.astype(BF16)
        e0_buf[t] = e0b
        o_t = dot_tn(values, e0b)
        o_buf[t] = o_t
        for c in range(4):
            d_buf[c, pl.ds(t, 1), :] = jnp.sum(dof_buf[c] * o_t, axis=0, keepdims=True)

    forward_tile(8)
    pass_on(0)
    forward_tile(9)
    pass_on(1)
    for t in range(2):
        mate_in[0, t].wait_recv()
        forward_tile(10 - 4 * core + t)
    for t in range(2):
        for d in (-1, 1):
            forward_tile(8 + 4 * d + t)
    pass_far(0)
    for t in range(2):
        for d in (-1, 1):
            mate_in[d, t].wait_recv()
            forward_tile(10 + 4 * d - 4 * core + t)
    pass_far(1)
    forward_tile(0)
    forward_tile(1)
    forward_tile(16)
    for t in range(2):
        mate_in[2, t].wait_recv()
        forward_tile(2 + 12 * core + t)

    m_all = m_buf[...]
    l_all = l_buf[...]
    big = jnp.zeros((TPAD, 128), F32)
    tt_in = []
    for c in range(4):
        z = m_all + bias_buf[c]
        top = jnp.max(z, axis=0, keepdims=True)
        ex = jnp.exp(z - top)
        mass = jnp.sum(ex * l_all, axis=0, keepdims=True)
        w_c = ex / mass
        w_buf[c] = w_c
        delta = jnp.sum(w_c * d_buf[c], axis=0, keepdims=True)
        big = big + w_c * delta
        tt_src[c] = w_c * (d_buf[c] - delta * l_all)
    for k in (1, 2, 3):
        there = (x + k) % 4
        tt_in.append(remote(tt_src.at[there], tt_buf.at[x], S_TT + k - 1, at_x(k)))
    tt_buf[x] = tt_src[x]

    dq_acc = jnp.zeros((128, 128), F32)

    def backward_slot(slot, dq_acc):
        for t in (2 * slot, 2 * slot + 1):
            if t >= NWIN:
                continue
            g_t = w_buf[0, t : t + 1, :] * dof_buf[0]
            for c in (1, 2, 3):
                g_t = g_t + w_buf[c, t : t + 1, :] * dof_buf[c]
            gb = g_t.astype(BF16)
            e0b = e0_buf[t]
            dp = dot_nn(kvw[t, :, 128:256], gb)
            ds = (e0b.astype(F32) * (dp - big[t : t + 1, :])).astype(BF16)
            dkvw[t, :, 0:128] = (dot_nn(ds, q_tile) * FACTOR).astype(BF16)
            dkvw[t, :, 128:256] = dot_nt(e0b, gb).astype(BF16)
            dq_acc = dq_acc + dot_tn(ds, kvw[t, :, 0:128])
        return dq_acc

    mate_in = {}
    def to_mate(slot, dq_acc):
        dq_acc = backward_slot(slot, dq_acc)
        j = slot // 2
        mate_in[j] = remote(
            dkvw.at[pl.ds(2 * slot, 2)], mate_dkv.at[j + 1], S_DKV + j, sibling
        )
        return dq_acc

    dq_acc = to_mate(1, dq_acc)
    dq_acc = to_mate(7, dq_acc)

    def chip_sum(e, t):
        return dkvw[4 * e + t].astype(F32) + mate_dkv[e + core, t].astype(F32)

    dq_acc = backward_slot(0, dq_acc)
    dq_acc = backward_slot(8, dq_acc)
    mate_in[0].wait_recv()
    mate_in[3].wait_recv()
    far = {}
    for t in range(2):
        for n, (e, d) in enumerate(((0, -1), (4, 1))):
            far_src[n, t] = chip_sum(e, t).astype(BF16)
            far[n, t] = remote(
                far_src.at[n, t],
                far_in.at[n, t],
                S_DFAR + 2 * t + n,
                at_seq(2 * d),
                chip_in(2 * d),
                chip_in(1) & chip_in(-1),
            )
    dq_acc = to_mate(3, dq_acc)
    dq_acc = to_mate(5, dq_acc)
    for slot in (2, 6, 4):
        dq_acc = backward_slot(slot, dq_acc)
    dq_x[x] = (dq_acc * FACTOR).astype(BF16)
    xq_in = [remote(dq_x.at[x], dq_x.at[x], S_XQ + k - 1, at_x(k)) for k in (1, 2, 3)]

    mate_in[1].wait_recv()
    mate_in[2].wait_recv()
    near = {}
    for t in range(2):
        for n, (e, d) in enumerate(((1, -1), (3, 1))):
            far[n, t].wait_recv()
            near_src[n, t] = (chip_sum(e, t) + far_in[n, t].astype(F32)).astype(BF16)
            near[n, t] = remote(
                near_src.at[n, t],
                near_in.at[n, t],
                S_DNEAR + 2 * t + n,
                at_seq(2 * d),
                chip_in(d),
                chip_in(-d),
            )

    for c in range(4):
        acc = jnp.zeros((128, 128), F32)
        for t in range(NWIN):
            acc = acc + w_buf[c, t : t + 1, :] * o_buf[t]
        att_src[c] = acc.T.astype(BF16)

    xkv_in = []
    for t in range(2):
        for n in range(2):
            near[n, t].wait_recv()
        acc = chip_sum(2, t) + near_in[0, t].astype(F32) + near_in[1, t].astype(F32)
        dkv_x[x, t] = acc.astype(BF16)
        xkv_in.append(
            [
                remote(
                    dkv_x.at[x, t], dkv_x.at[x, t], (S_XKV, S_XKV2)[t] + k - 1, at_x(k)
                )
                for k in (2, 1, 3)
            ]
        )

    for copy in tt_in:
        copy.wait_recv()
    ones = jnp.ones((8, 128), F32)
    rows = []
    for h in range(2):
        row = jnp.zeros((8, 128), F32)
        for r in range(2):
            sums = lax.dot_general(
                ones, tt_buf[2 * r + h], (((1,), (1,)), ((), ())),
                precision=lax.Precision.HIGHEST, preferred_element_type=F32,
            )
            row = row + lax.dot_general(
                sums, oh_buf[r], (((1,), (0,)), ((), ())),
                precision=lax.Precision.HIGHEST, preferred_element_type=F32,
            )
        rows.append(row)
    both_heads = rows[0] + pltpu.roll(rows[1], 32, axis=1)
    t_c[core] = both_heads
    tc_in = remote(t_c.at[core], t_c.at[core], S_TC, sibling)

    for copy in xq_in:
        copy.wait_recv()
    for t in range(2):
        for copy in xkv_in[t]:
            copy.wait_recv()
        at_rows = slice(128 * t, 128 * t + 128)
        for h in range(2):
            d3[0, at_rows, 128 * h : 128 * h + 128] = dq_x[2 * t + h]
            both = dkv_x[h, t].astype(F32) + dkv_x[2 + h, t].astype(F32)
            bothb = both.astype(BF16)
            d3[h, at_rows, 256 - 256 * h : 384 - 256 * h] = bothb[:, 0:128]
            d3[1, at_rows, 128 + 128 * h : 256 + 128 * h] = bothb[:, 128:256]

    att_in = []
    for k in (1, 2, 3):
        there = (x + k) % 4
        att_in.append(remote(att_src.at[there], att_buf.at[x], S_ATT + k - 1, at_x(k)))
    att_buf[x] = att_src[x]

    tc_in.wait_recv()
    t_y[y] = t_c[0] + t_c[1]
    ty_in = [remote(t_y.at[y], t_y.at[y], S_TY + k - 1, at_y(k)) for k in (1, 2, 3)]

    cross_in.wait_recv()
    halves = ((1 - zh, fcross, S_GC, S_GY), (zh, ft_ref, S_GC2, S_GY2))
    theirs = d3[1 - core]
    gc_in = []
    for part, rows_ref, slot, _ in halves:
        g_src[part] = dot_nn(rows_ref[...], theirs).astype(BF16)
        gc_in.append(remote(g_src.at[part], g_core.at[part], slot, sibling))
    mine = d3[core]
    gy_in = []
    for n, (part, rows_ref, _, slot) in enumerate(halves):
        product = dot_nn(rows_ref[...], mine)
        gc_in[n].wait_recv()
        g_c[part] = (product + g_core[part].astype(F32)).astype(BF16)
        for k in (2, 1, 3):
            there = (y + k) % 4
            gy_in.append(
                remote(
                    g_c.at[part, pl.ds(48 * there, 48)],
                    g_y.at[y, part],
                    slot + k - 1,
                    at_y(k),
                )
            )
        g_y[y, part] = g_c[part, pl.ds(48 * y, 48), :]

    for copy in ty_in:
        copy.wait_recv()
    t_z[z_lo] = (t_y[0] + t_y[1]) + (t_y[2] + t_y[3])
    tz_in = [
        remote(t_z.at[z_lo], t_z.at[z_lo], S_TZ + j - 1, at_near(j)) for j in (1, 2, 3)
    ]
    gz_in = []
    for n, (part, _, _, _) in enumerate(halves):
        for copy in gy_in[3 * n : 3 * n + 3]:
            copy.wait_recv()
        piece = g_y[0, part].astype(F32)
        for k in (1, 2, 3):
            piece = piece + g_y[k, part].astype(F32)
        g_zs[part] = piece.astype(BF16)
        for j in (0, 1, 3, 2) if n == 0 else (2, 1, 3):
            peer = at_far(j) if n == 0 else at_near(j)
            slot = S_GZ + j if n == 0 else S_GZ + 3 + j
            gz_in.append(remote(g_zs.at[part], g_z.at[zi], slot, peer))
    g_z[zi] = g_zs[zh]

    for copy in tz_in:
        copy.wait_recv()
    sums = ((t_z[0] + t_z[1]) + (t_z[2] + t_z[3]))[0:1, :]
    at_row = lax.broadcasted_iota(jnp.int32, (8, 128), 0)
    at_type = (lax.broadcasted_iota(jnp.int32, (8, 128), 1) == ids_ref[0]).astype(F32)
    t_x[zh, x] = jnp.where(at_row == 0, sums, jnp.where(at_row == 1, at_type, 0.0))
    tx_in = [remote(t_x.at[zh, x], t_x.at[zh, x], S_TX + k - 1, at_x(k)) for k in (1, 2, 3)]

    for copy in tx_in:
        copy.wait_recv()
    tcross_in = remote(t_x.at[zh], t_x.at[zh], S_TCROSS, antipode)

    for copy in gz_in:
        copy.wait_recv()
    piece = g_z[0].astype(F32)
    for k in range(1, 8):
        piece = piece + g_z[k].astype(F32)
    g_oy[y] = piece.astype(BF16)
    oy_in = [remote(g_oy.at[y], g_oy.at[y], S_OY + k - 1, at_y(k)) for k in (1, 2, 3)]
    oc_in = [remote(g_oy.at[y], g_oc.at[y], S_OC, sibling)]
    for copy in att_in:
        copy.wait_recv()
    for piece in range(4):
        r, h = piece // 2, piece % 2
        att_out[128 * r : 128 * r + 128, 128 * h : 128 * h + 128] = att_buf[piece]

    tcross_in.wait_recv()
    cells = [t_x[c // 4, c % 4] for c in range(8)]
    total = lax.dot_general(
        jnp.concatenate([tile[1:2] for tile in cells], axis=0),
        jnp.concatenate([tile[0:1] for tile in cells], axis=0),
        (((0,), (0,)), ((), ())),
        precision=lax.Precision.HIGHEST, preferred_element_type=F32,
    )
    table_out[...] = total[0:32]
    for k in (1, 3, 2):
        source = (y - k + 4) % 4
        oy_in[k - 1].wait_recv()
        oc_in.append(remote(g_oy.at[source], g_oc.at[source], S_OC2 + k - 1, sibling))
    for copy in oc_in:
        copy.wait_recv()
    grad_out[core] = g_oy[...]
    grad_out[1 - core] = g_oc[...]
    for copy in sends:
        copy.wait_send()


def finish(att_ref, pieces_ref, table_ref, att_out, grad_out, table_out):
    att_out[0] = att_ref[...]
    for k in range(2):
        for n in range(4):
            grad_out[48 * n : 48 * n + 48, 384 * k : 384 * k + 384] = pieces_ref[k, n].astype(F32)
    for h in range(2):
        table_out[:, h, :] = table_ref[:, 32 * h : 32 * h + 32]


def local(features, w_qkv, buckets, cell_ids, bias_table, d_attended):
    types, levels, _ = bias_table.shape
    vmem = pl.BlockSpec(memory_space=pltpu.VMEM)
    hbm = pl.BlockSpec(memory_space=pl.ANY)
    smem = pl.BlockSpec(memory_space=pltpu.SMEM)
    scratch = [
        pltpu.VMEM((192, 256), BF16),
        pltpu.VMEM((4, 96, 128), BF16),
        pltpu.VMEM((256, 256), BF16),
        pltpu.VMEM((32, 2, 32), F32),
        pltpu.VMEM((8, 128), F32),
        pltpu.VMEM((2, TPAD, 128), F32),
        pltpu.VMEM((4, TPAD, 128), F32),
        pltpu.VMEM((1536, 768), BF16),
        pltpu.VMEM((8, 96, 128), BF16),
        pltpu.VMEM((192, 256), BF16),
        pltpu.VMEM((4, 128, 128), BF16),
        pltpu.VMEM((4, 128, 128), BF16),
        pltpu.VMEM((4, TPAD, 128), F32),
        pltpu.VMEM((2, 64, 256), BF16),
        pltpu.VMEM((2, 64, 128), BF16),
        pltpu.VMEM((128, 128), BF16),
        pltpu.VMEM((18, 128, 256), BF16),
        pltpu.VMEM((NWIN, 128, 128), BF16),
        pltpu.VMEM((NWIN, 128, 128), F32),
        pltpu.VMEM((TPAD, 128), F32),
        pltpu.VMEM((TPAD, 128), F32),
        pltpu.VMEM((4, TPAD, 128), F32),
        pltpu.VMEM((4, TPAD, 128), F32),
        pltpu.VMEM((4, 128, 128), F32),
        pltpu.VMEM((4, 128, 128), BF16),
        pltpu.VMEM((4, 128, 128), BF16),
        pltpu.VMEM((4, TPAD, 128), F32),
        pltpu.VMEM((4, TPAD, 128), F32),
        pltpu.VMEM((18, 128, 256), BF16),
        pltpu.VMEM((6, 2, 128, 256), BF16),
        pltpu.VMEM((2, 2, 128, 256), BF16),
        pltpu.VMEM((2, 2, 128, 256), BF16),
        pltpu.VMEM((2, 2, 128, 256), BF16),
        pltpu.VMEM((2, 2, 128, 256), BF16),
        pltpu.VMEM((4, 2, 128, 256), BF16),
        pltpu.VMEM((4, 128, 128), BF16),
        pltpu.VMEM((2, 256, 384), BF16),
        pltpu.VMEM((2, 192, 384), BF16),
        pltpu.VMEM((2, 192, 384), BF16),
        pltpu.VMEM((2, 192, 384), BF16),
        pltpu.VMEM((4, 2, 48, 384), BF16),
        pltpu.VMEM((2, 48, 384), BF16),
        pltpu.VMEM((8, 48, 384), BF16),
        pltpu.VMEM((4, 48, 384), BF16),
        pltpu.VMEM((4, 48, 384), BF16),
        pltpu.VMEM((2, 8, 128), F32),
        pltpu.VMEM((4, 8, 128), F32),
        pltpu.VMEM((4, 8, 128), F32),
        pltpu.VMEM((2, 4, 8, 128), F32),
        pltpu.SemaphoreType.DMA((4,)),
        pltpu.SemaphoreType.DMA((N_SEM,)),
        pltpu.SemaphoreType.DMA((N_SEM,)),
    ]
    att, grad, table = pl.pallas_call(
        kernel,
        out_shape=(
            jax.ShapeDtypeStruct((256, 256), BF16),
            jax.ShapeDtypeStruct((2, 4, 48, 384), BF16),
            jax.ShapeDtypeStruct((types, 128), F32),
        ),
        in_specs=[hbm, hbm, smem, smem, hbm, hbm],
        out_specs=(vmem, vmem, vmem),
        scratch_shapes=scratch,
        compiler_params=pltpu.CompilerParams(collective_id=0, has_side_effects=True),
    )(features.T, w_qkv, buckets, cell_ids, bias_table.transpose(0, 2, 1), d_attended)
    att, grad, table = pl.pallas_call(
        finish,
        out_shape=(
            jax.ShapeDtypeStruct((1, 256, 256), BF16),
            jax.ShapeDtypeStruct((192, 768), F32),
            jax.ShapeDtypeStruct((types, HEADS, levels), F32),
        ),
        in_specs=[vmem] * 3,
        out_specs=(vmem,) * 3,
    )(att, grad, table)
    return (att, grad, table.transpose(0, 2, 1))


def solution(mesh):
    in_specs = (
        P("seq", "cell"),
        P(),
        P("cell", "seq", None),
        P("cell"),
        P(),
        P("cell", "seq", None),
    )
    out_specs = (P("cell", "seq", None), P("cell", None), P())
    return jax.shard_map(local, mesh=mesh, in_specs=in_specs, out_specs=out_specs, check_vma=False)
```
